256 devices in a mesh: case: 4 (over z_lo), span: 16 (over y, x), vert: 4 (over z_hi, core).
Axes of the slice: x: 4, y: 4, z: 8 (z_hi: 2, z_lo: 4; z = z_hi * 4 + z_lo), core: 2. Of those that a mesh axis runs over, the one named last changes fastest.
Arguments:
- state: float32 [8, 4, 128, 32, 512], P('case', None, 'span', 'vert'), may hold values from -3 to 4.5
- turbine_x: int32 [8, 6], P('case'), may hold values from 128 to 511
- turbine_y: int32 [8, 6], P('case'), may hold values from 0 to 127
- yaw_index: int32 [8], P('case'), may hold values from 0 to 7
Outputs:
- final_state: float32 [8, 4, 128, 32, 512], P('case', None, 'span', 'vert')
The draws below stay inside these ranges and needn't reach their ends.
All inputs are finite; a program needn't handle non-finite values.
Results may differ from the reference program's by a relative error of at most 0.0003.
Values sent between devices are 32-bit elements; how exact they have to be, the bound alone decides.
A program may use at most 64 MiB of HBM per device.

```python
import jax
import jax.numpy as jnp
from jax import lax

X = 512
FIELDS = 4
STEPS = 3
NT = 6
DISK = 8
DOM = 8
NY = 128
NZ = 32


def draw_state(key, part):
    shape = (DOM, FIELDS, NY, NZ, X)
    noise = 0.75 * jax.random.normal(key, shape, jnp.float32)
    noise = jnp.clip(noise, -3.0, 3.0)
    offset = jnp.array([0.0, 1.5, 0.0, 0.0], jnp.float32)[None, :, None, None, None]
    return noise + offset


def touch_ends(result, key, least, top_value):
    longest = result.shape.index(max(result.shape))
    spots = []
    for shift in (0, 1):
        where = [jax.random.randint(jax.random.fold_in(key, axis), (), 0, length) for axis, length in enumerate(result.shape)]
        where[longest] = (where[longest] + shift) % result.shape[longest]
        spots.append(tuple(where))
    return result.at[spots[0]].set(least).at[spots[1]].set(top_value)


def setup_inputs(seed: int = 0) -> dict:
    keys = jax.random.split(jax.random.key(seed), 5)
    return {
        "state": draw_state(jax.random.fold_in(keys[4], 71), 0),
        "turbine_x": touch_ends(jax.random.randint(keys[1], (DOM, NT), X // 4, X), jax.random.fold_in(keys[1], 1), X // 4, X - 1).astype(jnp.int32),
        "turbine_y": touch_ends(jax.random.randint(keys[2], (DOM, NT), 0, NY), jax.random.fold_in(keys[2], 1), 0, NY - 1).astype(jnp.int32),
        "yaw_index": touch_ends(jax.random.randint(keys[3], (DOM,), 0, 8), jax.random.fold_in(keys[3], 1), 0, 7).astype(jnp.int32),
    }


U_MEAN = 1.0
VISC = 0.04
THRUST = 0.75
TIME_STEP = 0.1
YAW_STEP = 0.15

def tendency(center, east, west, north, south, upper, lower, weight, cos_yaw, sin_yaw):
    grad_x = (east - west) * 0.5
    grad_y = (north - south) * 0.5
    grad_z = (upper - lower) * 0.5
    laplace = east + west + north + south + upper + lower - 6.0 * center
    vel_u = center[..., 1, :, :, :]
    vel_v = center[..., 2, :, :, :]
    vel_w = center[..., 3, :, :, :]
    dux = grad_x[..., 1, :, :, :]
    dvy = grad_y[..., 2, :, :, :]
    dwz = grad_z[..., 3, :, :, :]
    duy = grad_y[..., 1, :, :, :]
    duz = grad_z[..., 1, :, :, :]
    strain = dux * dux + dvy * dvy + dwz * dwz + duy * duy + duz * duz
    viscous = VISC * jnp.sqrt(1.0 + strain)
    speed = U_MEAN + vel_u
    flow = -(jnp.expand_dims(speed, -4) * grad_x + jnp.expand_dims(vel_v, -4) * grad_y + jnp.expand_dims(vel_w, -4) * grad_z)
    flow = flow + jnp.expand_dims(viscous, -4) * laplace
    normal = speed * cos_yaw + vel_v * sin_yaw
    thrust = THRUST * normal * jnp.abs(normal) * weight
    extra = jnp.stack([-(dux + dvy + dwz), -grad_x[..., 0, :, :, :] - thrust * cos_yaw, -grad_y[..., 0, :, :, :] - thrust * sin_yaw, -grad_z[..., 0, :, :, :]], axis=-4)
    return flow + extra

def neighbours(fields):
    east = jnp.roll(fields, -1, axis=3)
    west = jnp.roll(fields, 1, axis=3)
    north = jnp.roll(fields, -1, axis=1)
    south = jnp.roll(fields, 1, axis=1)
    padded = jnp.pad(fields, ((0, 0), (0, 0), (1, 1), (0, 0)))
    return (east, west, north, south, padded[:, :, 2:, :], padded[:, :, :-2, :])

def domain_step(fields, tx_row, ty_row, yaw, domain):
    along_x = jnp.arange(X, dtype=jnp.int32)
    along_y = jnp.arange(NY, dtype=jnp.int32)
    along_z = jnp.arange(NZ, dtype=jnp.int32)
    hit_x = (along_x[None, :] == tx_row[:, None]).astype(jnp.float32)
    hit_y = ((along_y[None, :] - ty_row[:, None]) % NY < DISK).astype(jnp.float32)
    plane = jnp.dot(hit_y.T, hit_x, precision=lax.Precision.HIGHEST)
    lower_half = (along_z < NZ // 2).astype(jnp.float32)
    active = (domain > 0).astype(jnp.float32)
    weight = plane[:, None, :] * lower_half[None, :, None] * active
    angle = (yaw.astype(jnp.float32) - 3.5) * YAW_STEP
    cos_yaw = jnp.cos(angle)
    sin_yaw = jnp.sin(angle)

    def rate(values):
        return tendency(values, *neighbours(values), weight, cos_yaw, sin_yaw)
    first = rate(fields)
    middle = fields + TIME_STEP * first
    second = rate(middle)
    return fields + 0.5 * TIME_STEP * (first + second)

def reference(state, turbine_x, turbine_y, yaw_index):
    width = X // 4
    ramp = 0.5 * (1.0 - jnp.cos(jnp.pi * (jnp.arange(width, dtype=jnp.float32) + 1.0) / width))
    domains = jnp.arange(DOM, dtype=jnp.int32)
    for step in range(STEPS):
        state = lax.map(lambda items: domain_step(*items), (state, turbine_x, turbine_y, yaw_index, domains))
        front = state[..., :width]
        source = front[0:1]
        front = front + ramp * (source - front)
        state = jnp.concatenate([front, state[..., width:]], axis=4)
    return state
```

```python
import functools
import math

import jax
import jax.numpy as jnp
from jax import lax
from jax.experimental import pallas as pl
from jax.experimental.pallas import tpu as pltpu
from jax.sharding import PartitionSpec as P

STEPS = 3
DISK = 8
VISC = 0.04
THRUST = 0.75
TIME_STEP = 0.1
YAW_STEP = 0.15
MESH = pl.DeviceIdType.MESH

OWN = slice(2, 6)


def roll_s(v, shift):
    return pltpu.roll(v, shift % 8, 0)


def kernel(
    state_ref, tx_ref, ty_ref, yaw_ref, out_ref,
    stage, q, mid, send_z, recv_z, recv_c, fringe, weight, angle_cos, angle_sin, ramp_ref,
    load_sem, hs, hr, fs, fr,
):
    case, span, vert = lax.axis_index("case"), lax.axis_index("span"), lax.axis_index("vert")
    n_case, n_span, n_vert = lax.axis_size("case"), lax.axis_size("span"), lax.axis_size("vert")
    left, right = lax.rem(span + n_span - 1, n_span), lax.rem(span + 1, n_span)
    below, above = lax.rem(vert + n_vert - 1, n_vert), lax.rem(vert + 1, n_vert)
    has_below, has_above = vert > 0, vert < n_vert - 1
    total_y, half_z = 8 * n_span, 4 * n_vert

    loads = [
        pltpu.make_async_copy(state_ref.at[u], stage.at[u], load_sem.at[u]) for u in (0, 1)
    ]
    for copy in loads:
        copy.start()

    barrier = pltpu.get_barrier_semaphore()
    partners = [
        {"span": s, "vert": v} for s in (left, span, right) for v in (below, vert, above)
    ]
    partners.pop(4)
    partners += [
        {"case": lax.rem(case + 1, n_case)},
        {"case": lax.rem(case + n_case - 1, n_case)},
    ]
    for partner in partners:
        pl.semaphore_signal(barrier, inc=1, device_id=partner, device_id_type=MESH)

    sub = lax.broadcasted_iota(jnp.int32, (8, 128), 0)
    lane = lax.broadcasted_iota(jnp.int32, (8, 128), 1)
    low_half = (sub & 1) == 0
    first_lane, last_lane = lane == 0, lane == 127
    along_x = (sub >> 1) * 128 + lane

    wave = jnp.cos((math.pi / 128.0) * (along_x + 1).astype(jnp.float32))
    ramp_ref[...] = jnp.where(sub < 2, 0.5 * (1.0 - wave), 0.0)
    zeros = jnp.zeros((8, 128), jnp.float32)
    half = jnp.where(low_half, 0, 4)
    for u in (0, 1):
        yaw = jnp.full((8, 128), yaw_ref[u], jnp.int32).astype(jnp.float32)
        angle = (yaw - 3.5) * YAW_STEP
        angle_cos[u] = jnp.cos(angle)
        angle_sin[u] = jnp.sin(angle)

        @pl.loop(1, 11)
        def _(row):
            y = span * 8 + row - 2
            total = zeros
            for k in range(tx_ref.shape[1]):
                offset = jnp.full((8, 128), y - ty_ref[u, k], jnp.int32) & (total_y - 1)
                hit = (along_x == tx_ref[u, k]) & (offset < DISK)
                total = total + jnp.where(hit, THRUST, 0.0)
            domain = jnp.full((8, 128), 2 * case + u, jnp.int32)
            for kind, z in enumerate((1, 2, 6)):
                height = half + (vert * 8 + z - 2)
                weight[u, kind, row] = jnp.where((height < half_z) & (domain > 0), total, 0.0)

    @pl.when(jnp.logical_not(has_below))
    def _():
        @pl.loop(0, 8)
        def _(y):
            for par in (0, 1):
                for u in (0, 1):
                    for f in range(4):
                        recv_z[par, u, 0, f, y] = zeros
        for par in (0, 1):
            for u in (0, 1):
                for f in range(4):
                    recv_c[par, u, 0, f] = zeros
                    recv_c[par, u, 2, f] = zeros

    @pl.when(jnp.logical_not(has_above))
    def _():
        @pl.loop(0, 8)
        def _(y):
            for par in (0, 1):
                for u in (0, 1):
                    for f in range(4):
                        recv_z[par, u, 1, f, y] = zeros
        for par in (0, 1):
            for u in (0, 1):
                for f in range(4):
                    recv_c[par, u, 1, f] = zeros
                    recv_c[par, u, 3, f] = zeros

    def remote(src, dst, par, u, k, device):
        return pltpu.make_async_remote_copy(
            src_ref=src, dst_ref=dst, send_sem=hs.at[par, u, k], recv_sem=hr.at[par, u, k],
            device_id=device, device_id_type=MESH,
        )

    def halo_copies(par, u):
        own = q.at[par, u]
        return [
            (remote(own.at[:, 9, 5], recv_c.at[par, u, 0], par, u, 4, {"span": right, "vert": above}), has_above, has_below),
            (remote(own.at[:, 9, 2], recv_c.at[par, u, 1], par, u, 5, {"span": right, "vert": below}), has_below, has_above),
            (remote(own.at[:, 2, 5], recv_c.at[par, u, 2], par, u, 6, {"span": left, "vert": above}), has_above, has_below),
            (remote(own.at[:, 2, 2], recv_c.at[par, u, 3], par, u, 7, {"span": left, "vert": below}), has_below, has_above),
            (remote(send_z.at[par, u, 0], recv_z.at[par, u, 0], par, u, 2, {"vert": above}), has_above, has_below),
            (remote(send_z.at[par, u, 1], recv_z.at[par, u, 1], par, u, 3, {"vert": below}), has_below, has_above),
            (remote(own.at[:, 8:10, OWN], own.at[:, 0:2, OWN], par, u, 0, {"span": right}), None, None),
            (remote(own.at[:, 2:4, OWN], own.at[:, 10:12, OWN], par, u, 1, {"span": left}), None, None),
        ]

    def guarded(condition, action):
        if condition is None:
            action()
        else:
            pl.when(condition)(action)

    def send_halos(par, u):
        @pl.loop(0, 8)
        def _(y):
            for f in range(4):
                z0, z1, z2, z3 = (q[par, u, f, y + 2, z] for z in range(2, 6))
                send_z[par, u, 0, f, y] = jnp.where(low_half, roll_s(z2, -1), z3)
                send_z[par, u, 1, f, y] = jnp.where(low_half, z0, roll_s(z1, 1))

        for copy, sends, _ in halo_copies(par, u):
            guarded(sends, copy.start)

    def receive_halos(par, u):
        for copy, _, receives in halo_copies(par, u):
            guarded(receives, copy.wait_recv)

        @pl.loop(0, 8)
        def _(y):
            for f in range(4):
                z0, z1, z2, z3 = (q[par, u, f, y + 2, z] for z in range(2, 6))
                low, high = recv_z[par, u, 0, f, y], recv_z[par, u, 1, f, y]
                q[par, u, f, y + 2, 0] = jnp.where(low_half, low, roll_s(z2, 1))
                q[par, u, f, y + 2, 1] = jnp.where(low_half, roll_s(low, -1), roll_s(z3, 1))
                q[par, u, f, y + 2, 6] = jnp.where(low_half, roll_s(z0, -1), roll_s(high, 1))
                q[par, u, f, y + 2, 7] = jnp.where(low_half, roll_s(z1, -1), high)

        for f in range(4):
            for row, low, high in ((1, 0, 1), (10, 2, 3)):
                low, high = recv_c[par, u, low, f], recv_c[par, u, high, f]
                q[par, u, f, row, 1] = jnp.where(low_half, roll_s(low, -1), roll_s(q[par, u, f, row, 5], 1))
                q[par, u, f, row, 6] = jnp.where(low_half, roll_s(q[par, u, f, row, 2], -1), roll_s(high, 1))

    def sent_halos(par, u):
        for copy, sends, _ in halo_copies(par, u):
            guarded(sends, copy.wait_send)

    def tendency(ref, u, row, z, cos, sin):
        center, gx, gy, gz, laplace = [], [], [], [], []
        for f in range(4):
            c = ref[f, row, z]
            north, south = ref[f, row + 1, z], ref[f, row - 1, z]
            upper, lower = ref[f, row, z + 1], ref[f, row, z - 1]
            east, west = pltpu.roll(c, 127, 1), pltpu.roll(c, 1, 1)
            east = jnp.where(last_lane, roll_s(east, -2), east)
            west = jnp.where(first_lane, roll_s(west, 2), west)
            center.append(c)
            gx.append(east - west)
            gy.append(north - south)
            gz.append(upper - lower)
            laplace.append(((east + west) + (north + south)) + (upper + lower) - 6.0 * c)
        strain = gx[1] * gx[1] + gy[2] * gy[2] + gz[3] * gz[3] + gy[1] * gy[1] + gz[1] * gz[1]
        viscous = (0.5 * VISC) * jnp.sqrt(4.0 + strain)
        speed = 1.0 + center[1]
        half_u, half_v, half_w = 0.5 * speed, 0.5 * center[2], 0.5 * center[3]
        normal = speed * cos + center[2] * sin
        kind = 0 if z == 1 else 2 if z == 6 else 1
        thrust = normal * jnp.abs(normal) * weight[u, kind, row]
        extra = [
            0.5 * (gx[1] + gy[2] + gz[3]),
            0.5 * gx[0] + thrust * cos,
            0.5 * gy[0] + thrust * sin,
            0.5 * gz[0],
        ]
        rates = [
            viscous * laplace[f] - (half_u * gx[f] + half_v * gy[f] + half_w * gz[f] + extra[f])
            for f in range(4)
        ]
        return center, rates

    def advance(par, nxt, u):
        cos, sin = angle_cos[u], angle_sin[u]
        field = q.at[par, u]

        def first(row, zs):
            for z in zs:
                center, rates = tendency(field, u, row, z, cos, sin)
                for f in range(4):
                    value = center[f] + TIME_STEP * rates[f]
                    if z == 1:
                        value = jnp.where(low_half & edge_low, 0.0, value)
                    if z == 6:
                        value = jnp.where(jnp.logical_not(low_half) & edge_high, 0.0, value)
                    mid[f, row, z] = value

        edge_low = jnp.full((8, 128), vert, jnp.int32) == 0
        edge_high = jnp.full((8, 128), vert, jnp.int32) == n_vert - 1

        @pl.loop(0, 2)
        def _(side):
            first(1 + 9 * side, range(2, 6))

        @pl.loop(2, 10)
        def _(row):
            first(row, range(1, 7))

        sent_halos(par, u)

        @pl.loop(2, 10)
        def _(row):
            for z in range(2, 6):
                center, rates = tendency(mid, u, row, z, cos, sin)
                for f in range(4):
                    q[nxt, u, f, row, z] = 0.5 * (field[f, row, z] + center[f]) + (0.5 * TIME_STEP) * rates[f]

    def blend(nxt, u, s):
        ramp = ramp_ref[...]

        @pl.loop(0, 8)
        def _(y):
            for f in range(4):
                packed = fringe[s, f, y]
                for k in range(4):
                    value = q[nxt, u, f, y + 2, 2 + k]
                    q[nxt, u, f, y + 2, 2 + k] = value + ramp * (roll_s(packed, -2 * k) - value)

    def fringe_copy(s, f):
        return pltpu.make_async_remote_copy(
            src_ref=fringe.at[s, f], dst_ref=fringe.at[s, f], send_sem=fs.at[s, f], recv_sem=fr.at[s, f],
            device_id={"case": lax.rem(case + 1, n_case)}, device_id_type=MESH,
        )

    def pack_fringe(nxt, s):
        for f in range(4):
            @pl.loop(0, 8)
            def _(y):
                parts = [roll_s(q[nxt, 0, f, y + 2, 2 + k], 2 * k) if k else q[nxt, 0, f, y + 2, 2] for k in range(4)]
                fringe[s, f, y] = jnp.where(
                    sub < 4, jnp.where(sub < 2, parts[0], parts[1]), jnp.where(sub < 6, parts[2], parts[3])
                )

            fringe_copy(s, f).start()

    def emit(nxt, u):
        @pl.loop(0, 8)
        def _(y):
            for f in range(4):
                for k in range(4):
                    out_ref[u, f, y, pl.ds(k, 8, stride=4), :] = q[nxt, u, f, y + 2, 2 + k]

    for u in (0, 1):
        loads[u].wait()

        @pl.loop(0, 8)
        def _(y):
            for f in range(4):
                for k in range(4):
                    q[0, u, f, y + 2, 2 + k] = stage[u, f, y, pl.ds(k, 8, stride=4), :]

        if u == 0:
            pl.semaphore_wait(barrier, len(partners))
        send_halos(0, u)

    @pl.loop(0, STEPS)
    def _(s):
        par = lax.rem(s, 2)
        nxt = 1 - par
        more = s < STEPS - 1
        receive_halos(par, 0)
        advance(par, nxt, 0)

        @pl.when(case == 0)
        def _():
            pack_fringe(nxt, s)

        @pl.when((case == 0) & more)
        def _():
            send_halos(nxt, 0)

        receive_halos(par, 1)
        advance(par, nxt, 1)

        @pl.when(case > 0)
        def _():
            for f in range(4):
                fringe_copy(s, f).wait_recv()
                pl.when(case < n_case - 1)(fringe_copy(s, f).start)
            blend(nxt, 0, s)

        @pl.when((case > 0) & more)
        def _():
            send_halos(nxt, 0)

        blend(nxt, 1, s)

        @pl.when(more)
        def _():
            send_halos(nxt, 1)

        @pl.when(case < n_case - 1)
        def _():
            for f in range(4):
                fringe_copy(s, f).wait_send()

    for u in (0, 1):
        emit(STEPS % 2, u)


def body(state, turbine_x, turbine_y, yaw_index):
    slots, fields, rows_y, rows_z, x = state.shape
    tiles = x // 128
    tiled = state.reshape(slots, fields, rows_y, rows_z, tiles, 128).transpose(0, 1, 2, 4, 3, 5)
    tiled = tiled.reshape(slots, fields, rows_y, tiles * rows_z, 128)
    domain = (2, 4, 12, 8, 8, 128)
    out = pl.pallas_call(
        kernel,
        out_shape=jax.ShapeDtypeStruct(tiled.shape, jnp.float32),
        in_specs=[pl.BlockSpec(memory_space=pl.ANY)] + [pl.BlockSpec(memory_space=pltpu.SMEM)] * 3,
        out_specs=pl.BlockSpec(memory_space=pltpu.VMEM),
        scratch_shapes=[
            pltpu.VMEM(tiled.shape, jnp.float32),
            pltpu.VMEM((2,) + domain, jnp.float32),
            pltpu.VMEM(domain[1:], jnp.float32),
            pltpu.VMEM((2, 2, 2, 4, 8, 8, 128), jnp.float32),
            pltpu.VMEM((2, 2, 2, 4, 8, 8, 128), jnp.float32),
            pltpu.VMEM((2, 2, 4, 4, 8, 128), jnp.float32),
            pltpu.VMEM((STEPS, 4, 8, 8, 128), jnp.float32),
            pltpu.VMEM((2, 3, 12, 8, 128), jnp.float32),
            pltpu.VMEM((2, 8, 128), jnp.float32),
            pltpu.VMEM((2, 8, 128), jnp.float32),
            pltpu.VMEM((8, 128), jnp.float32),
            pltpu.SemaphoreType.DMA((2,)),
            pltpu.SemaphoreType.DMA((2, 2, 8)),
            pltpu.SemaphoreType.DMA((2, 2, 8)),
            pltpu.SemaphoreType.DMA((STEPS, 4)),
            pltpu.SemaphoreType.DMA((STEPS, 4)),
        ],
        compiler_params=pltpu.CompilerParams(
            collective_id=0, has_side_effects=True, vmem_limit_bytes=40 << 20
        ),
        name="heun_steps",
    )(tiled, turbine_x, turbine_y, yaw_index)
    out = out.reshape(slots, fields, rows_y, tiles, rows_z, 128).transpose(0, 1, 2, 4, 3, 5)
    return out.reshape(state.shape)


def solution(mesh):
    return jax.shard_map(
        body,
        mesh=mesh,
        in_specs=(
            P("case", None, "span", "vert", None),
            P("case", None),
            P("case", None),
            P("case"),
        ),
        out_specs=P("case", None, "span", "vert", None),
        check_vma=False,
    )
```

```python
import functools
import math

import jax
import jax.numpy as jnp
from jax import lax
from jax.experimental import pallas as pl
from jax.experimental.pallas import tpu as pltpu
from jax.sharding import PartitionSpec as P

STEPS = 3
DISK = 8
VISC = 0.04
THRUST = 0.75
TIME_STEP = 0.1
YAW_STEP = 0.15
MESH = pl.DeviceIdType.MESH

OWN = slice(2, 6)


def roll_s(v, shift):
    return pltpu.roll(v, shift % 8, 0)


def kernel(
    state_ref, tx_hbm, ty_hbm, yaw_hbm, out_ref,
    stage, q, mid, send_z, recv_z, recv_c, fringe, weight, angle_cos, angle_sin, ramp_ref, tx_ref, ty_ref, yaw_ref,
    load_sem, hs, hr, fs, fr,
):
    case, span, vert = lax.axis_index("case"), lax.axis_index("span"), lax.axis_index("vert")
    n_case, n_span, n_vert = lax.axis_size("case"), lax.axis_size("span"), lax.axis_size("vert")
    left, right = lax.rem(span + n_span - 1, n_span), lax.rem(span + 1, n_span)
    below, above = lax.rem(vert + n_vert - 1, n_vert), lax.rem(vert + 1, n_vert)
    has_below, has_above = vert > 0, vert < n_vert - 1
    total_y, half_z = 8 * n_span, 4 * n_vert

    loads = [
        pltpu.make_async_copy(state_ref.at[u], stage.at[u], load_sem.at[u]) for u in (0, 1)
    ]
    loads += [
        pltpu.make_async_copy(src, dst, load_sem.at[2 + i])
        for i, (src, dst) in enumerate(((tx_hbm, tx_ref), (ty_hbm, ty_ref), (yaw_hbm, yaw_ref)))
    ]
    for copy in loads:
        copy.start()

    barrier = pltpu.get_barrier_semaphore()
    partners = [
        {"span": s, "vert": v} for s in (left, span, right) for v in (below, vert, above)
    ]
    partners.pop(4)
    partners += [
        {"case": lax.rem(case + k, n_case)} for k in range(1, 4)
    ]
    for partner in partners:
        pl.semaphore_signal(barrier, inc=1, device_id=partner, device_id_type=MESH)

    sub = lax.broadcasted_iota(jnp.int32, (8, 128), 0)
    lane = lax.broadcasted_iota(jnp.int32, (8, 128), 1)
    low_half = (sub & 1) == 0
    first_lane, last_lane = lane == 0, lane == 127
    along_x = (sub >> 1) * 128 + lane

    zeros = jnp.zeros((8, 128), jnp.float32)

    def constants():
        for copy in loads[2:]:
            copy.wait()
        wave = jnp.cos((math.pi / 128.0) * (along_x + 1).astype(jnp.float32))
        ramp_ref[...] = jnp.where(sub < 2, 0.5 * (1.0 - wave), 0.0)
        half = jnp.where(low_half, 0, 4)
        for u in (0, 1):
            yaw = jnp.full((8, 128), yaw_ref[u], jnp.int32).astype(jnp.float32)
            angle = (yaw - 3.5) * YAW_STEP
            angle_cos[u] = jnp.cos(angle)
            angle_sin[u] = jnp.sin(angle)

            @pl.loop(1, 11)
            def _(row):
                y = span * 8 + row - 2
                total = zeros
                for k in range(tx_ref.shape[1]):
                    offset = jnp.full((8, 128), y - ty_ref[u, k], jnp.int32) & (total_y - 1)
                    hit = (along_x == tx_ref[u, k]) & (offset < DISK)
                    total = total + jnp.where(hit, THRUST, 0.0)
                domain = jnp.full((8, 128), 2 * case + u, jnp.int32)
                for kind, z in enumerate((1, 2, 6)):
                    height = half + (vert * 8 + z - 2)
                    weight[u, kind, row] = jnp.where((height < half_z) & (domain > 0), total, 0.0)

        @pl.when(jnp.logical_not(has_below))
        def _():
            @pl.loop(0, 4)
            def _(y):
                for par in (0, 1):
                    for u in (0, 1):
                        for f in range(4):
                            recv_z[par, u, 0, 0, f, y] = zeros
                            recv_z[par, u, 0, 1, f, y] = zeros
            for par in (0, 1):
                for u in (0, 1):
                    for f in range(4):
                        recv_c[par, u, 0, f] = zeros
                        recv_c[par, u, 2, f] = zeros

        @pl.when(jnp.logical_not(has_above))
        def _():
            @pl.loop(0, 4)
            def _(y):
                for par in (0, 1):
                    for u in (0, 1):
                        for f in range(4):
                            recv_z[par, u, 1, 0, f, y] = zeros
                            recv_z[par, u, 1, 1, f, y] = zeros
            for par in (0, 1):
                for u in (0, 1):
                    for f in range(4):
                        recv_c[par, u, 1, f] = zeros
                        recv_c[par, u, 3, f] = zeros

    def remote(src, dst, par, u, k, device):
        return pltpu.make_async_remote_copy(
            src_ref=src, dst_ref=dst, send_sem=hs.at[par, u, k], recv_sem=hr.at[par, u, k],
            device_id=device, device_id_type=MESH,
        )

    def halo_copies(par, u, part):
        own = q.at[par, u]
        if part == "corner":
            return [
                (remote(own.at[:, 9, 5], recv_c.at[par, u, 0], par, u, 4, {"span": right, "vert": above}), has_above, has_below),
                (remote(own.at[:, 9, 2], recv_c.at[par, u, 1], par, u, 5, {"span": right, "vert": below}), has_below, has_above),
                (remote(own.at[:, 2, 5], recv_c.at[par, u, 2], par, u, 6, {"span": left, "vert": above}), has_above, has_below),
                (remote(own.at[:, 2, 2], recv_c.at[par, u, 3], par, u, 7, {"span": left, "vert": below}), has_below, has_above),
            ]
        if part == "inner":
            return [
                (remote(send_z.at[par, u, 0, 0], recv_z.at[par, u, 0, 0], par, u, 0, {"vert": above}), has_above, has_below),
                (remote(send_z.at[par, u, 1, 0], recv_z.at[par, u, 1, 0], par, u, 1, {"vert": below}), has_below, has_above),
                (remote(own.at[:, 9, OWN], own.at[:, 1, OWN], par, u, 2, {"span": right}), None, None),
                (remote(own.at[:, 2, OWN], own.at[:, 10, OWN], par, u, 3, {"span": left}), None, None),
            ]
        return [
            (remote(send_z.at[par, u, 0, 1], recv_z.at[par, u, 0, 1], par, u, 8, {"vert": above}), has_above, has_below),
            (remote(send_z.at[par, u, 1, 1], recv_z.at[par, u, 1, 1], par, u, 9, {"vert": below}), has_below, has_above),
            (remote(own.at[:, 8, OWN], own.at[:, 0, OWN], par, u, 10, {"span": right}), None, None),
            (remote(own.at[:, 3, OWN], own.at[:, 11, OWN], par, u, 11, {"span": left}), None, None),
        ]

    def guarded(condition, action):
        if condition is None:
            action()
        else:
            pl.when(condition)(action)

    def send_halos(par, u):
        for copy, sends, _ in halo_copies(par, u, "corner"):
            guarded(sends, copy.start)

        @pl.loop(0, 4)
        def _(y):
            for f in range(4):
                even = [q[par, u, f, 2 * y + 2, z] for z in range(2, 6)]
                odd = [q[par, u, f, 2 * y + 3, z] for z in range(2, 6)]
                send_z[par, u, 0, 0, f, y] = jnp.where(low_half, roll_s(even[3], -1), odd[3])
                send_z[par, u, 0, 1, f, y] = jnp.where(low_half, roll_s(even[2], -1), odd[2])
                send_z[par, u, 1, 0, f, y] = jnp.where(low_half, even[0], roll_s(odd[0], 1))
                send_z[par, u, 1, 1, f, y] = jnp.where(low_half, even[1], roll_s(odd[1], 1))

        for copy, sends, _ in halo_copies(par, u, "inner") + halo_copies(par, u, "outer"):
            guarded(sends, copy.start)

    def merge_z(par, u, layer):
        @pl.loop(0, 4)
        def _(y):
            for f in range(4):
                low, high = recv_z[par, u, 0, layer, f, y], recv_z[par, u, 1, layer, f, y]
                for odd in (0, 1):
                    row = 2 * y + 2 + odd
                    near_low, near_high = q[par, u, f, row, 5 - layer], q[par, u, f, row, 2 + layer]
                    q[par, u, f, row, 1 - layer] = jnp.where(low_half, roll_s(low, -1) if odd else low, roll_s(near_low, 1))
                    q[par, u, f, row, 6 + layer] = jnp.where(low_half, roll_s(near_high, -1), high if odd else roll_s(high, 1))

    def receive_inner(par, u):
        for copy, _, receives in halo_copies(par, u, "inner"):
            guarded(receives, copy.wait_recv)
        merge_z(par, u, 0)

    def receive_outer(par, u):
        for copy, _, receives in halo_copies(par, u, "outer"):
            guarded(receives, copy.wait_recv)
        merge_z(par, u, 1)

    def receive_corners(par, u):
        for copy, _, receives in halo_copies(par, u, "corner"):
            guarded(receives, copy.wait_recv)
        for f in range(4):
            for row, low, high in ((1, 0, 1), (10, 2, 3)):
                low, high = recv_c[par, u, low, f], recv_c[par, u, high, f]
                q[par, u, f, row, 1] = jnp.where(low_half, roll_s(low, -1), roll_s(q[par, u, f, row, 5], 1))
                q[par, u, f, row, 6] = jnp.where(low_half, roll_s(q[par, u, f, row, 2], -1), roll_s(high, 1))

    def sent_halos(par, u):
        for part in ("corner", "inner", "outer"):
            for copy, sends, _ in halo_copies(par, u, part):
                guarded(sends, copy.wait_send)

    def tendency(ref, u, row, z, cos, sin):
        center, gx, gy, gz, laplace = [], [], [], [], []
        for f in range(4):
            c = ref[f, row, z]
            north, south = ref[f, row + 1, z], ref[f, row - 1, z]
            upper, lower = ref[f, row, z + 1], ref[f, row, z - 1]
            east, west = pltpu.roll(c, 127, 1), pltpu.roll(c, 1, 1)
            east = jnp.where(last_lane, roll_s(east, -2), east)
            west = jnp.where(first_lane, roll_s(west, 2), west)
            center.append(c)
            gx.append(east - west)
            gy.append(north - south)
            gz.append(upper - lower)
            laplace.append(((east + west) + (north + south)) + (upper + lower) - 6.0 * c)
        strain = gx[1] * gx[1] + gy[2] * gy[2] + gz[3] * gz[3] + gy[1] * gy[1] + gz[1] * gz[1]
        viscous = (0.5 * VISC) * jnp.sqrt(4.0 + strain)
        speed = 1.0 + center[1]
        half_u, half_v, half_w = 0.5 * speed, 0.5 * center[2], 0.5 * center[3]
        normal = speed * cos + center[2] * sin
        kind = 0 if z == 1 else 2 if z == 6 else 1
        thrust = normal * jnp.abs(normal) * weight[u, kind, row]
        extra = [
            0.5 * (gx[1] + gy[2] + gz[3]),
            0.5 * gx[0] + thrust * cos,
            0.5 * gy[0] + thrust * sin,
            0.5 * gz[0],
        ]
        rates = [
            viscous * laplace[f] - (half_u * gx[f] + half_v * gy[f] + half_w * gz[f] + extra[f])
            for f in range(4)
        ]
        return center, rates

    def advance(par, nxt, u, s):
        cos, sin = angle_cos[u], angle_sin[u]
        field = q.at[par, u]

        def first(row, zs):
            for z in zs:
                center, rates = tendency(field, u, row, z, cos, sin)
                for f in range(4):
                    value = center[f] + TIME_STEP * rates[f]
                    if z == 1:
                        value = jnp.where(low_half & edge_low, 0.0, value)
                    if z == 6:
                        value = jnp.where(jnp.logical_not(low_half) & edge_high, 0.0, value)
                    mid[f, row, z] = value

        edge_low = jnp.full((8, 128), vert, jnp.int32) == 0
        edge_high = jnp.full((8, 128), vert, jnp.int32) == n_vert - 1

        @pl.loop(3, 9, step=3)
        def _(row):
            for r in range(3):
                first(row + r, (3, 4))

        receive_inner(par, u)

        first(2, range(2, 6))
        first(9, range(2, 6))

        @pl.loop(3, 9, step=3)
        def _(row):
            for r in range(3):
                first(row + r, (2, 5))

        receive_outer(par, u)

        first(1, (3, 4))
        first(10, (3, 4))

        @pl.loop(3, 9, step=3)
        def _(row):
            for r in range(3):
                first(row + r, (1, 6))

        def second(row, zs):
            for z in zs:
                center, rates = tendency(mid, u, row, z, cos, sin)
                for f in range(4):
                    q[nxt, u, f, row, z] = 0.5 * (field[f, row, z] + center[f]) + (0.5 * TIME_STEP) * rates[f]

        pl.when(s > 0)(lambda: sent_halos(1 - par, u))

        @pl.loop(3, 9, step=2)
        def _(row):
            second(row, range(2, 6))
            second(row + 1, range(2, 6))

        second(2, (3, 4))
        second(9, (3, 4))

        receive_corners(par, u)

        for row, z in ((1, 2), (1, 5), (10, 2), (10, 5), (2, 1), (2, 6), (9, 1), (9, 6)):
            first(row, (z,))
        for row, z in ((2, 2), (2, 5), (9, 2), (9, 5)):
            second(row, (z,))

    def blend(nxt, u, s):
        ramp = ramp_ref[...]

        @pl.loop(0, 8)
        def _(y):
            for f in range(4):
                packed = fringe[s, f, y]
                for k in range(4):
                    value = q[nxt, u, f, y + 2, 2 + k]
                    q[nxt, u, f, y + 2, 2 + k] = value + ramp * (roll_s(packed, -2 * k) - value)

    def fringe_copy(s, f, k=1):
        return pltpu.make_async_remote_copy(
            src_ref=fringe.at[s, f], dst_ref=fringe.at[s, f], send_sem=fs.at[s, f, k], recv_sem=fr.at[s, f],
            device_id={"case": lax.rem(case + k, n_case)}, device_id_type=MESH,
        )

    def pack_fringe(nxt, s):
        for f in range(4):
            @pl.loop(0, 8)
            def _(y):
                parts = [roll_s(q[nxt, 0, f, y + 2, 2 + k], 2 * k) if k else q[nxt, 0, f, y + 2, 2] for k in range(4)]
                fringe[s, f, y] = jnp.where(
                    sub < 4, jnp.where(sub < 2, parts[0], parts[1]), jnp.where(sub < 6, parts[2], parts[3])
                )

            fringe_copy(s, f, 2).start()
            fringe_copy(s, f, 1).start()

    def emit(nxt, u):
        @pl.loop(0, 8)
        def _(y):
            for f in range(4):
                for k in range(4):
                    out_ref[u, f, y, pl.ds(k, 8, stride=4), :] = q[nxt, u, f, y + 2, 2 + k]

    for u in (0, 1):
        loads[u].wait()

        @pl.loop(0, 8)
        def _(y):
            for f in range(4):
                for k in range(4):
                    q[0, u, f, y + 2, 2 + k] = stage[u, f, y, pl.ds(k, 8, stride=4), :]

        if u == 0:
            pl.semaphore_wait(barrier, len(partners))
        send_halos(0, u)

    constants()

    @pl.loop(0, STEPS)
    def _(s):
        par = lax.rem(s, 2)
        nxt = 1 - par
        more = s < STEPS - 1
        advance(par, nxt, 0, s)

        @pl.when(case == 0)
        def _():
            pack_fringe(nxt, s)

        @pl.when((case == 0) & more)
        def _():
            send_halos(nxt, 0)

        def finish_first():
            for f in range(4):
                fringe_copy(s, f).wait_recv()
                pl.when(case == 2)(fringe_copy(s, f).start)
            blend(nxt, 0, s)

            @pl.when(more)
            def _():
                send_halos(nxt, 0)

        pl.when((case > 0) & (s > 0))(finish_first)

        advance(par, nxt, 1, s)

        pl.when((case > 0) & (s == 0))(finish_first)

        blend(nxt, 1, s)

        @pl.when(more)
        def _():
            send_halos(nxt, 1)

        @pl.when(case == 0)
        def _():
            for f in range(4):
                for k in (1, 2):
                    fringe_copy(s, f, k).wait_send()

        @pl.when(case == 2)
        def _():
            for f in range(4):
                fringe_copy(s, f).wait_send()

    for u in (0, 1):
        emit(STEPS % 2, u)
    for u in (0, 1):
        sent_halos((STEPS - 1) % 2, u)


def body(state, turbine_x, turbine_y, yaw_index):
    slots, fields, rows_y, rows_z, x = state.shape
    tiles = x // 128
    tiled = state.reshape(slots, fields, rows_y, rows_z, tiles, 128).transpose(0, 1, 2, 4, 3, 5)
    tiled = tiled.reshape(slots, fields, rows_y, tiles * rows_z, 128)
    domain = (2, 4, 12, 8, 8, 128)
    out = pl.pallas_call(
        kernel,
        out_shape=jax.ShapeDtypeStruct(tiled.shape, jnp.float32),
        in_specs=[pl.BlockSpec(memory_space=pltpu.HBM)] + [pl.BlockSpec(memory_space=pltpu.HBM)] * 3,
        out_specs=pl.BlockSpec(memory_space=pltpu.VMEM),
        scratch_shapes=[
            pltpu.VMEM(tiled.shape, jnp.float32),
            pltpu.VMEM((2,) + domain, jnp.float32),
            pltpu.VMEM(domain[1:], jnp.float32),
            pltpu.VMEM((2, 2, 2, 2, 4, 4, 8, 128), jnp.float32),
            pltpu.VMEM((2, 2, 2, 2, 4, 4, 8, 128), jnp.float32),
            pltpu.VMEM((2, 2, 4, 4, 8, 128), jnp.float32),
            pltpu.VMEM((STEPS, 4, 8, 8, 128), jnp.float32),
            pltpu.VMEM((2, 3, 12, 8, 128), jnp.float32),
            pltpu.VMEM((2, 8, 128), jnp.float32),
            pltpu.VMEM((2, 8, 128), jnp.float32),
            pltpu.VMEM((8, 128), jnp.float32),
            pltpu.SMEM(turbine_x.shape, jnp.int32),
            pltpu.SMEM(turbine_y.shape, jnp.int32),
            pltpu.SMEM(yaw_index.shape, jnp.int32),
            pltpu.SemaphoreType.DMA((5,)),
            pltpu.SemaphoreType.DMA((2, 2, 12)),
            pltpu.SemaphoreType.DMA((2, 2, 12)),
            pltpu.SemaphoreType.DMA((STEPS, 4, 4)),
            pltpu.SemaphoreType.DMA((STEPS, 4)),
        ],
        compiler_params=pltpu.CompilerParams(
            collective_id=0, has_side_effects=True, vmem_limit_bytes=60 << 20
        ),
        name="heun_steps",
    )(tiled, turbine_x, turbine_y, yaw_index)
    out = out.reshape(slots, fields, rows_y, tiles, rows_z, 128).transpose(0, 1, 2, 4, 3, 5)
    return out.reshape(state.shape)


def solution(mesh):
    return jax.shard_map(
        body,
        mesh=mesh,
        in_specs=(
            P("case", None, "span", "vert", None),
            P("case", None),
            P("case", None),
            P("case"),
        ),
        out_specs=P("case", None, "span", "vert", None),
        check_vma=False,
    )
```

```python
import functools
import math

import jax
import jax.numpy as jnp
from jax import lax
from jax.experimental import pallas as pl
from jax.experimental.pallas import tpu as pltpu
from jax.sharding import PartitionSpec as P

STEPS = 3
DISK = 8
VISC = 0.04
THRUST = 0.75
TIME_STEP = 0.1
YAW_STEP = 0.15
MESH = pl.DeviceIdType.MESH

OWN = slice(2, 6)


def roll_s(v, shift):
    return pltpu.roll(v, shift % 8, 0)


def kernel(
    state_ref, tx_hbm, ty_hbm, yaw_hbm, out_ref,
    stage, q, mid, send_z, recv_z, send_c, recv_c, fringe, weight, angle_cos, angle_sin, ramp_ref, tx_ref, ty_ref, yaw_ref,
    load_sem, hs, hr, fs, fr,
):
    case, span, vert = lax.axis_index("case"), lax.axis_index("span"), lax.axis_index("vert")
    n_case, n_span, n_vert = lax.axis_size("case"), lax.axis_size("span"), lax.axis_size("vert")
    left, right = lax.rem(span + n_span - 1, n_span), lax.rem(span + 1, n_span)
    below, above = lax.rem(vert + n_vert - 1, n_vert), lax.rem(vert + 1, n_vert)
    has_below, has_above = vert > 0, vert < n_vert - 1
    total_y, half_z = 8 * n_span, 4 * n_vert

    loads = [
        pltpu.make_async_copy(state_ref.at[u], stage.at[u], load_sem.at[u]) for u in (0, 1)
    ]
    loads += [
        pltpu.make_async_copy(src, dst, load_sem.at[2 + i])
        for i, (src, dst) in enumerate(((tx_hbm, tx_ref), (ty_hbm, ty_ref), (yaw_hbm, yaw_ref)))
    ]
    for copy in loads:
        copy.start()

    barrier = pltpu.get_barrier_semaphore()
    partners = [
        {"span": s, "vert": v} for s in (left, span, right) for v in (below, vert, above)
    ]
    partners.pop(4)
    partners += [
        {"case": lax.rem(case + k, n_case)} for k in range(1, 4)
    ]
    for partner in partners:
        pl.semaphore_signal(barrier, inc=1, device_id=partner, device_id_type=MESH)

    sub = lax.broadcasted_iota(jnp.int32, (8, 128), 0)
    lane = lax.broadcasted_iota(jnp.int32, (8, 128), 1)
    low_half = (sub & 1) == 0
    first_lane, last_lane = lane == 0, lane == 127
    along_x = (sub >> 1) * 128 + lane

    zeros = jnp.zeros((8, 128), jnp.float32)

    def constants():
        for copy in loads[2:]:
            copy.wait()
        wave = jnp.cos((math.pi / 128.0) * (along_x + 1).astype(jnp.float32))
        ramp_ref[...] = jnp.where(sub < 2, 0.5 * (1.0 - wave), 0.0)
        half = jnp.where(low_half, 0, 4)
        for u in (0, 1):
            yaw = jnp.full((8, 128), yaw_ref[u], jnp.int32).astype(jnp.float32)
            angle = (yaw - 3.5) * YAW_STEP
            angle_cos[u] = jnp.cos(angle)
            angle_sin[u] = jnp.sin(angle)

            @pl.loop(1, 11)
            def _(row):
                y = span * 8 + row - 2
                total = zeros
                for k in range(tx_ref.shape[1]):
                    offset = jnp.full((8, 128), y - ty_ref[u, k], jnp.int32) & (total_y - 1)
                    hit = (along_x == tx_ref[u, k]) & (offset < DISK)
                    total = total + jnp.where(hit, THRUST, 0.0)
                domain = jnp.full((8, 128), 2 * case + u, jnp.int32)
                for kind, z in enumerate((1, 2, 6)):
                    height = half + (vert * 8 + z - 2)
                    weight[u, kind, row] = jnp.where((height < half_z) & (domain > 0), total, 0.0)

        @pl.when(jnp.logical_not(has_below))
        def _():
            @pl.loop(0, 4)
            def _(y):
                for par in (0, 1):
                    for u in (0, 1):
                        for f in range(4):
                            recv_z[par, u, 0, 0, f, y] = zeros
                            recv_z[par, u, 0, 1, f, y] = zeros
            for par in (0, 1):
                for u in (0, 1):
                    for f in range(2):
                        recv_c[par, u, 0, f] = zeros
                        recv_c[par, u, 2, f] = zeros

        @pl.when(jnp.logical_not(has_above))
        def _():
            @pl.loop(0, 4)
            def _(y):
                for par in (0, 1):
                    for u in (0, 1):
                        for f in range(4):
                            recv_z[par, u, 1, 0, f, y] = zeros
                            recv_z[par, u, 1, 1, f, y] = zeros
            for par in (0, 1):
                for u in (0, 1):
                    for f in range(2):
                        recv_c[par, u, 1, f] = zeros
                        recv_c[par, u, 3, f] = zeros

    def remote(src, dst, par, u, k, device):
        return pltpu.make_async_remote_copy(
            src_ref=src, dst_ref=dst, send_sem=hs.at[par, u, k], recv_sem=hr.at[par, u, k],
            device_id=device, device_id_type=MESH,
        )

    def halo_copies(par, u, part):
        own = q.at[par, u]
        if part == "corner":
            return [
                (remote(send_c.at[par, u, 0], recv_c.at[par, u, 0], par, u, 4, {"span": right, "vert": above}), has_above, has_below),
                (remote(send_c.at[par, u, 1], recv_c.at[par, u, 1], par, u, 5, {"span": right, "vert": below}), has_below, has_above),
                (remote(send_c.at[par, u, 2], recv_c.at[par, u, 2], par, u, 6, {"span": left, "vert": above}), has_above, has_below),
                (remote(send_c.at[par, u, 3], recv_c.at[par, u, 3], par, u, 7, {"span": left, "vert": below}), has_below, has_above),
            ]
        if part == "inner":
            return [
                (remote(send_z.at[par, u, 0, 0], recv_z.at[par, u, 0, 0], par, u, 0, {"vert": above}), has_above, has_below),
                (remote(send_z.at[par, u, 1, 0], recv_z.at[par, u, 1, 0], par, u, 1, {"vert": below}), has_below, has_above),
                (remote(own.at[:, 9, OWN], own.at[:, 1, OWN], par, u, 2, {"span": right}), None, None),
                (remote(own.at[:, 2, OWN], own.at[:, 10, OWN], par, u, 3, {"span": left}), None, None),
            ]
        return [
            (remote(send_z.at[par, u, 0, 1], recv_z.at[par, u, 0, 1], par, u, 8, {"vert": above}), has_above, has_below),
            (remote(send_z.at[par, u, 1, 1], recv_z.at[par, u, 1, 1], par, u, 9, {"vert": below}), has_below, has_above),
            (remote(own.at[:, 8, OWN], own.at[:, 0, OWN], par, u, 10, {"span": right}), None, None),
            (remote(own.at[:, 3, OWN], own.at[:, 11, OWN], par, u, 11, {"span": left}), None, None),
        ]

    def guarded(condition, action):
        if condition is None:
            action()
        else:
            pl.when(condition)(action)

    def send_halos(par, u):
        for k, (row, z) in enumerate(((9, 5), (9, 2), (2, 5), (2, 2))):
            for f in (0, 2):
                even, odd = q[par, u, f, row, z], q[par, u, f + 1, row, z]
                pair = (roll_s(even, -1), odd) if z == 5 else (even, roll_s(odd, 1))
                send_c[par, u, k, f // 2] = jnp.where(low_half, *pair)
        for copy, sends, _ in halo_copies(par, u, "corner"):
            guarded(sends, copy.start)

        @pl.loop(0, 4)
        def _(y):
            for f in range(4):
                even = [q[par, u, f, 2 * y + 2, z] for z in range(2, 6)]
                odd = [q[par, u, f, 2 * y + 3, z] for z in range(2, 6)]
                send_z[par, u, 0, 0, f, y] = jnp.where(low_half, roll_s(even[3], -1), odd[3])
                send_z[par, u, 0, 1, f, y] = jnp.where(low_half, roll_s(even[2], -1), odd[2])
                send_z[par, u, 1, 0, f, y] = jnp.where(low_half, even[0], roll_s(odd[0], 1))
                send_z[par, u, 1, 1, f, y] = jnp.where(low_half, even[1], roll_s(odd[1], 1))

        for copy, sends, _ in halo_copies(par, u, "inner") + halo_copies(par, u, "outer"):
            guarded(sends, copy.start)

    def merge_z(par, u, layer):
        @pl.loop(0, 4)
        def _(y):
            for f in range(4):
                low, high = recv_z[par, u, 0, layer, f, y], recv_z[par, u, 1, layer, f, y]
                for odd in (0, 1):
                    row = 2 * y + 2 + odd
                    near_low, near_high = q[par, u, f, row, 5 - layer], q[par, u, f, row, 2 + layer]
                    q[par, u, f, row, 1 - layer] = jnp.where(low_half, roll_s(low, -1) if odd else low, roll_s(near_low, 1))
                    q[par, u, f, row, 6 + layer] = jnp.where(low_half, roll_s(near_high, -1), high if odd else roll_s(high, 1))

    def receive_inner(par, u):
        for copy, _, receives in halo_copies(par, u, "inner"):
            guarded(receives, copy.wait_recv)
        merge_z(par, u, 0)

    def receive_outer(par, u):
        for copy, _, receives in halo_copies(par, u, "outer"):
            guarded(receives, copy.wait_recv)
        merge_z(par, u, 1)

    def receive_corners(par, u):
        for copy, _, receives in halo_copies(par, u, "corner"):
            guarded(receives, copy.wait_recv)
        for f in range(4):
            for row, low, high in ((1, 0, 1), (10, 2, 3)):
                near_low, near_high = recv_c[par, u, low, f // 2], recv_c[par, u, high, f // 2]
                if f % 2:
                    near_low = roll_s(near_low, -1)
                else:
                    near_high = roll_s(near_high, 1)
                q[par, u, f, row, 1] = jnp.where(low_half, near_low, roll_s(q[par, u, f, row, 5], 1))
                q[par, u, f, row, 6] = jnp.where(low_half, roll_s(q[par, u, f, row, 2], -1), near_high)

    def sent_halos(par, u):
        for part in ("corner", "inner", "outer"):
            for copy, sends, _ in halo_copies(par, u, part):
                guarded(sends, copy.wait_send)

    def tendency(ref, u, row, z, cos, sin):
        center, gx, gy, gz, laplace = [], [], [], [], []
        for f in range(4):
            c = ref[f, row, z]
            north, south = ref[f, row + 1, z], ref[f, row - 1, z]
            upper, lower = ref[f, row, z + 1], ref[f, row, z - 1]
            east, west = pltpu.roll(c, 127, 1), pltpu.roll(c, 1, 1)
            east = jnp.where(last_lane, roll_s(east, -2), east)
            west = jnp.where(first_lane, roll_s(west, 2), west)
            center.append(c)
            gx.append(east - west)
            gy.append(north - south)
            gz.append(upper - lower)
            laplace.append(((east + west) + (north + south)) + (upper + lower) - 6.0 * c)
        strain = gx[1] * gx[1] + gy[2] * gy[2] + gz[3] * gz[3] + gy[1] * gy[1] + gz[1] * gz[1]
        viscous = (0.5 * VISC) * jnp.sqrt(4.0 + strain)
        speed = 1.0 + center[1]
        half_u, half_v, half_w = 0.5 * speed, 0.5 * center[2], 0.5 * center[3]
        normal = speed * cos + center[2] * sin
        kind = 0 if z == 1 else 2 if z == 6 else 1
        thrust = normal * jnp.abs(normal) * weight[u, kind, row]
        extra = [
            0.5 * (gx[1] + gy[2] + gz[3]),
            0.5 * gx[0] + thrust * cos,
            0.5 * gy[0] + thrust * sin,
            0.5 * gz[0],
        ]
        rates = [
            viscous * laplace[f] - (half_u * gx[f] + half_v * gy[f] + half_w * gz[f] + extra[f])
            for f in range(4)
        ]
        return center, rates

    def fringe_copy(s, chunk):
        part = fringe.at[s, pl.ds(*((1, 3), (4, 3), (0, 1), (7, 1))[chunk])]
        return pltpu.make_async_remote_copy(
            src_ref=part, dst_ref=part, send_sem=fs.at[s, chunk], recv_sem=fr.at[s, chunk],
            device_id={"case": lax.rem(case + 1, n_case)}, device_id_type=MESH,
        )

    def pack_fringe(nxt, s, start, stop, step, chunks):
        @pl.loop(start, stop, step=step)
        def _(y):
            for f in range(4):
                parts = [q[nxt, 0, f, y + 2, 2 + k] for k in range(4)]
                parts = [parts[0]] + [roll_s(parts[k], 2 * k) for k in (1, 2, 3)]
                fringe[s, y, f] = jnp.where(
                    sub < 4, jnp.where(sub < 2, parts[0], parts[1]), jnp.where(sub < 6, parts[2], parts[3])
                )

        for chunk in chunks:
            fringe_copy(s, chunk).start()

    def advance(par, nxt, u, s):
        cos, sin = angle_cos[u], angle_sin[u]
        field = q.at[par, u]

        def first(row, zs):
            for z in zs:
                center, rates = tendency(field, u, row, z, cos, sin)
                for f in range(4):
                    value = center[f] + TIME_STEP * rates[f]
                    if z == 1:
                        value = jnp.where(low_half & edge_low, 0.0, value)
                    if z == 6:
                        value = jnp.where(jnp.logical_not(low_half) & edge_high, 0.0, value)
                    mid[f, row, z] = value

        edge_low = jnp.full((8, 128), vert, jnp.int32) == 0
        edge_high = jnp.full((8, 128), vert, jnp.int32) == n_vert - 1

        @pl.loop(3, 9, step=3)
        def _(row):
            for r in range(3):
                first(row + r, (3, 4))

        receive_inner(par, u)

        first(2, range(2, 6))
        first(9, range(2, 6))

        @pl.loop(3, 9, step=3)
        def _(row):
            for r in range(3):
                first(row + r, (2, 5))

        receive_outer(par, u)

        first(1, (3, 4))
        first(10, (3, 4))

        @pl.loop(3, 9, step=3)
        def _(row):
            for r in range(3):
                first(row + r, (1, 6))

        def second(row, zs):
            for z in zs:
                center, rates = tendency(mid, u, row, z, cos, sin)
                for f in range(4):
                    q[nxt, u, f, row, z] = 0.5 * (field[f, row, z] + center[f]) + (0.5 * TIME_STEP) * rates[f]

        pl.when((s > 0) & ((u == 1) | (s != 1)))(lambda: sent_halos(1 - par, u))

        @pl.loop(3, 9, step=2)
        def _(row):
            second(row, range(2, 6))
            second(row + 1, range(2, 6))

        @pl.when((case == 0) & (u == 0))
        def _():
            pack_fringe(nxt, s, 1, 7, 1, (0, 1))

        second(2, (3, 4))
        second(9, (3, 4))

        receive_corners(par, u)

        for row, z in ((1, 2), (1, 5), (10, 2), (10, 5), (2, 1), (2, 6), (9, 1), (9, 6)):
            first(row, (z,))
        for row, z in ((2, 2), (2, 5), (9, 2), (9, 5)):
            second(row, (z,))

    def blend(nxt, u, s):
        ramp = ramp_ref[...]

        @pl.loop(0, 8)
        def _(y):
            for f in range(4):
                packed = fringe[s, y, f]
                for k in range(4):
                    value = q[nxt, u, f, y + 2, 2 + k]
                    q[nxt, u, f, y + 2, 2 + k] = value + ramp * (roll_s(packed, -2 * k) - value)

    def emit(nxt, u):
        @pl.loop(0, 8)
        def _(y):
            for f in range(4):
                for k in range(4):
                    out_ref[u, f, y, pl.ds(k, 8, stride=4), :] = q[nxt, u, f, y + 2, 2 + k]

    for u in (0, 1):
        loads[u].wait()

        @pl.loop(0, 8)
        def _(y):
            for f in range(4):
                for k in range(4):
                    q[0, u, f, y + 2, 2 + k] = stage[u, f, y, pl.ds(k, 8, stride=4), :]

        if u == 0:
            pl.semaphore_wait(barrier, len(partners))
        if u == 1:
            sent_halos(0, 0)
        send_halos(0, u)

    constants()

    ahead = ((0, 0), (1, 0), (0, 1), (1, 1), (0, 2), (1, 2))

    @pl.loop(0, 2 * STEPS)
    def _(task):
        u, s = lax.rem(task, 2), lax.div(task, 2)
        for spot, (slot, step) in enumerate(ahead):
            here = (case == 0) & (task == spot)
            u, s = jnp.where(here, slot, u), jnp.where(here, step, s)
        par = lax.rem(s, 2)
        nxt = 1 - par
        more = s < STEPS - 1
        first_slot = u == 0
        early = ((s > 0) | (case == 1)) & ((s < STEPS - 1) | (case < n_case - 1))

        advance(par, nxt, u, s)

        @pl.when((case == 0) & first_slot)
        def _():
            pack_fringe(nxt, s, 0, 8, 7, (2, 3))

        @pl.when((case > 0) & (first_slot == early))
        def _():
            for f in range(4):
                fringe_copy(s, f).wait_recv()
                pl.when(case < n_case - 1)(fringe_copy(s, f).start)
            blend(nxt, 0, s)

        @pl.when(more & ((case == 0) & first_slot | (case > 0) & (first_slot == early)))
        def _():
            send_halos(nxt, 0)

        @pl.when(jnp.logical_not(first_slot))
        def _():
            blend(nxt, 1, s)
            pl.when(more)(lambda: send_halos(nxt, 1))

    @pl.when(case < n_case - 1)
    def _():
        for s in range(STEPS):
            for f in range(4):
                fringe_copy(s, f).wait_send()

    for u in (0, 1):
        emit(STEPS % 2, u)
    for u in (0, 1):
        sent_halos((STEPS - 1) % 2, u)


def body(state, turbine_x, turbine_y, yaw_index):
    slots, fields, rows_y, rows_z, x = state.shape
    tiles = x // 128
    tiled = state.reshape(slots, fields, rows_y, rows_z, tiles, 128).transpose(0, 1, 2, 4, 3, 5)
    tiled = tiled.reshape(slots, fields, rows_y, tiles * rows_z, 128)
    domain = (2, 4, 12, 8, 8, 128)
    out = pl.pallas_call(
        kernel,
        out_shape=jax.ShapeDtypeStruct(tiled.shape, jnp.float32),
        in_specs=[pl.BlockSpec(memory_space=pltpu.HBM)] + [pl.BlockSpec(memory_space=pltpu.HBM)] * 3,
        out_specs=pl.BlockSpec(memory_space=pltpu.VMEM),
        scratch_shapes=[
            pltpu.VMEM(tiled.shape, jnp.float32),
            pltpu.VMEM((2,) + domain, jnp.float32),
            pltpu.VMEM(domain[1:], jnp.float32),
            pltpu.VMEM((2, 2, 2, 2, 4, 4, 8, 128), jnp.float32),
            pltpu.VMEM((2, 2, 2, 2, 4, 4, 8, 128), jnp.float32),
            pltpu.VMEM((2, 2, 4, 2, 8, 128), jnp.float32),
            pltpu.VMEM((2, 2, 4, 2, 8, 128), jnp.float32),
            pltpu.VMEM((STEPS, 8, 4, 8, 128), jnp.float32),
            pltpu.VMEM((2, 3, 12, 8, 128), jnp.float32),
            pltpu.VMEM((2, 8, 128), jnp.float32),
            pltpu.VMEM((2, 8, 128), jnp.float32),
            pltpu.VMEM((8, 128), jnp.float32),
            pltpu.SMEM(turbine_x.shape, jnp.int32),
            pltpu.SMEM(turbine_y.shape, jnp.int32),
            pltpu.SMEM(yaw_index.shape, jnp.int32),
            pltpu.SemaphoreType.DMA((5,)),
            pltpu.SemaphoreType.DMA((2, 2, 12)),
            pltpu.SemaphoreType.DMA((2, 2, 12)),
            pltpu.SemaphoreType.DMA((STEPS, 4)),
            pltpu.SemaphoreType.DMA((STEPS, 4)),
        ],
        compiler_params=pltpu.CompilerParams(
            collective_id=0, has_side_effects=True, vmem_limit_bytes=60 << 20
        ),
        name="heun_steps",
    )(tiled, turbine_x, turbine_y, yaw_index)
    out = out.reshape(slots, fields, rows_y, tiles, rows_z, 128).transpose(0, 1, 2, 4, 3, 5)
    return out.reshape(state.shape)


def solution(mesh):
    return jax.shard_map(
        body,
        mesh=mesh,
        in_specs=(
            P("case", None, "span", "vert", None),
            P("case", None),
            P("case", None),
            P("case"),
        ),
        out_specs=P("case", None, "span", "vert", None),
        check_vma=False,
    )
```

```python
import functools
import math

import jax
import jax.numpy as jnp
from jax import lax
from jax.experimental import pallas as pl
from jax.experimental.pallas import tpu as pltpu
from jax.sharding import PartitionSpec as P

STEPS = 3
DISK = 8
VISC = 0.04
THRUST = 0.75
TIME_STEP = 0.1
YAW_STEP = 0.15
MESH = pl.DeviceIdType.MESH

OWN = slice(2, 6)


def roll_s(v, shift):
    return pltpu.roll(v, shift % 8, 0)


def kernel(
    state_ref, tx_hbm, ty_hbm, yaw_hbm, out_ref,
    stage, q, mid, send_z, recv_z, send_c, recv_c, fringe, weight, angle_cos, angle_sin, ramp_ref, tx_ref, ty_ref, yaw_ref,
    load_sem, hs, hr, fs, fr,
):
    case, span, vert = lax.axis_index("case"), lax.axis_index("span"), lax.axis_index("vert")
    n_case, n_span, n_vert = lax.axis_size("case"), lax.axis_size("span"), lax.axis_size("vert")
    left, right = lax.rem(span + n_span - 1, n_span), lax.rem(span + 1, n_span)
    below, above = lax.rem(vert + n_vert - 1, n_vert), lax.rem(vert + 1, n_vert)
    has_below, has_above = vert > 0, vert < n_vert - 1
    total_y, half_z = 8 * n_span, 4 * n_vert

    loads = [
        pltpu.make_async_copy(state_ref.at[u], stage.at[u], load_sem.at[u]) for u in (0, 1)
    ]
    loads += [
        pltpu.make_async_copy(src, dst, load_sem.at[2 + i])
        for i, (src, dst) in enumerate(((tx_hbm, tx_ref), (ty_hbm, ty_ref), (yaw_hbm, yaw_ref)))
    ]
    barrier = pltpu.get_barrier_semaphore()
    partners = [
        {"span": s, "vert": v} for s in (left, span, right) for v in (below, vert, above)
    ]
    partners.pop(4)
    partners += [{"case": lax.rem(case + k, n_case)} for k in (1, n_case - 1)]
    for partner in partners:
        pl.semaphore_signal(barrier, inc=1, device_id=partner, device_id_type=MESH)
    for copy in loads:
        copy.start()

    sub = lax.broadcasted_iota(jnp.int32, (8, 128), 0)
    lane = lax.broadcasted_iota(jnp.int32, (8, 128), 1)
    low_half = (sub & 1) == 0
    first_lane, last_lane = lane == 0, lane == 127
    along_x = (sub >> 1) * 128 + lane

    zeros = jnp.zeros((8, 128), jnp.float32)

    def constants():
        for copy in loads[2:]:
            copy.wait()
        wave = jnp.cos((math.pi / 128.0) * (along_x + 1).astype(jnp.float32))
        ramp_ref[...] = jnp.where(sub < 2, 0.5 * (1.0 - wave), 0.0)
        half = jnp.where(low_half, 0, 4)
        for u in (0, 1):
            yaw = jnp.full((8, 128), yaw_ref[u], jnp.int32).astype(jnp.float32)
            angle = (yaw - 3.5) * YAW_STEP
            angle_cos[u] = jnp.cos(angle)
            angle_sin[u] = jnp.sin(angle)

            @pl.loop(1, 11)
            def _(row):
                y = span * 8 + row - 2
                total = zeros
                for k in range(tx_ref.shape[1]):
                    offset = jnp.full((8, 128), y - ty_ref[u, k], jnp.int32) & (total_y - 1)
                    hit = (along_x == tx_ref[u, k]) & (offset < DISK)
                    total = total + jnp.where(hit, THRUST, 0.0)
                domain = jnp.full((8, 128), 2 * case + u, jnp.int32)
                for kind, z in enumerate((1, 2, 6)):
                    height = half + (vert * 8 + z - 2)
                    weight[u, kind, row] = jnp.where((height < half_z) & (domain > 0), total, 0.0)

        @pl.when(jnp.logical_not(has_below))
        def _():
            @pl.loop(0, 4)
            def _(y):
                for par in (0, 1):
                    for u in (0, 1):
                        for f in range(4):
                            recv_z[par, u, 0, 0, f, y] = zeros
                            recv_z[par, u, 0, 1, f, y] = zeros
            for par in (0, 1):
                for u in (0, 1):
                    for f in range(2):
                        recv_c[par, u, 0, f] = zeros
                        recv_c[par, u, 2, f] = zeros

        @pl.when(jnp.logical_not(has_above))
        def _():
            @pl.loop(0, 4)
            def _(y):
                for par in (0, 1):
                    for u in (0, 1):
                        for f in range(4):
                            recv_z[par, u, 1, 0, f, y] = zeros
                            recv_z[par, u, 1, 1, f, y] = zeros
            for par in (0, 1):
                for u in (0, 1):
                    for f in range(2):
                        recv_c[par, u, 1, f] = zeros
                        recv_c[par, u, 3, f] = zeros

    def remote(src, dst, par, u, k, device):
        return pltpu.make_async_remote_copy(
            src_ref=src, dst_ref=dst, send_sem=hs.at[par, u, k], recv_sem=hr.at[par, u, k],
            device_id=device, device_id_type=MESH,
        )

    def halo_copies(par, u, part):
        own = q.at[par, u]
        if part == "corner":
            return [
                (remote(send_c.at[par, u, 0], recv_c.at[par, u, 0], par, u, 4, {"span": right, "vert": above}), has_above, has_below),
                (remote(send_c.at[par, u, 1], recv_c.at[par, u, 1], par, u, 5, {"span": right, "vert": below}), has_below, has_above),
                (remote(send_c.at[par, u, 2], recv_c.at[par, u, 2], par, u, 6, {"span": left, "vert": above}), has_above, has_below),
                (remote(send_c.at[par, u, 3], recv_c.at[par, u, 3], par, u, 7, {"span": left, "vert": below}), has_below, has_above),
            ]
        if part == "inner":
            return [
                (remote(send_z.at[par, u, 0, 0], recv_z.at[par, u, 0, 0], par, u, 0, {"vert": above}), has_above, has_below),
                (remote(send_z.at[par, u, 1, 0], recv_z.at[par, u, 1, 0], par, u, 1, {"vert": below}), has_below, has_above),
                (remote(own.at[:, 9, OWN], own.at[:, 1, OWN], par, u, 2, {"span": right}), None, None),
                (remote(own.at[:, 2, OWN], own.at[:, 10, OWN], par, u, 3, {"span": left}), None, None),
            ]
        return [
            (remote(send_z.at[par, u, 0, 1], recv_z.at[par, u, 0, 1], par, u, 8, {"vert": above}), has_above, has_below),
            (remote(send_z.at[par, u, 1, 1], recv_z.at[par, u, 1, 1], par, u, 9, {"vert": below}), has_below, has_above),
            (remote(own.at[:, 8, OWN], own.at[:, 0, OWN], par, u, 10, {"span": right}), None, None),
            (remote(own.at[:, 3, OWN], own.at[:, 11, OWN], par, u, 11, {"span": left}), None, None),
        ]

    def guarded(condition, action):
        if condition is None:
            action()
        else:
            pl.when(condition)(action)

    def send_halos(par, u):
        for k, (row, z) in enumerate(((9, 5), (9, 2), (2, 5), (2, 2))):
            for f in (0, 2):
                even, odd = q[par, u, f, row, z], q[par, u, f + 1, row, z]
                pair = (roll_s(even, -1), odd) if z == 5 else (even, roll_s(odd, 1))
                send_c[par, u, k, f // 2] = jnp.where(low_half, *pair)
        for copy, sends, _ in halo_copies(par, u, "corner"):
            guarded(sends, copy.start)

        @pl.loop(0, 4)
        def _(y):
            for f in range(4):
                even = [q[par, u, f, 2 * y + 2, z] for z in range(2, 6)]
                odd = [q[par, u, f, 2 * y + 3, z] for z in range(2, 6)]
                send_z[par, u, 0, 0, f, y] = jnp.where(low_half, roll_s(even[3], -1), odd[3])
                send_z[par, u, 0, 1, f, y] = jnp.where(low_half, roll_s(even[2], -1), odd[2])
                send_z[par, u, 1, 0, f, y] = jnp.where(low_half, even[0], roll_s(odd[0], 1))
                send_z[par, u, 1, 1, f, y] = jnp.where(low_half, even[1], roll_s(odd[1], 1))

        for copy, sends, _ in halo_copies(par, u, "inner") + halo_copies(par, u, "outer"):
            guarded(sends, copy.start)

    def merge_z(par, u, layer):
        @pl.loop(0, 4)
        def _(y):
            for f in range(4):
                low, high = recv_z[par, u, 0, layer, f, y], recv_z[par, u, 1, layer, f, y]
                for odd in (0, 1):
                    row = 2 * y + 2 + odd
                    near_low, near_high = q[par, u, f, row, 5 - layer], q[par, u, f, row, 2 + layer]
                    q[par, u, f, row, 1 - layer] = jnp.where(low_half, roll_s(low, -1) if odd else low, roll_s(near_low, 1))
                    q[par, u, f, row, 6 + layer] = jnp.where(low_half, roll_s(near_high, -1), high if odd else roll_s(high, 1))

    def receive_inner(par, u):
        for copy, _, receives in halo_copies(par, u, "inner"):
            guarded(receives, copy.wait_recv)
        merge_z(par, u, 0)

    def receive_outer(par, u):
        for copy, _, receives in halo_copies(par, u, "outer"):
            guarded(receives, copy.wait_recv)
        merge_z(par, u, 1)

    def receive_corners(par, u):
        for copy, _, receives in halo_copies(par, u, "corner"):
            guarded(receives, copy.wait_recv)
        for f in range(4):
            for row, low, high in ((1, 0, 1), (10, 2, 3)):
                near_low, near_high = recv_c[par, u, low, f // 2], recv_c[par, u, high, f // 2]
                if f % 2:
                    near_low = roll_s(near_low, -1)
                else:
                    near_high = roll_s(near_high, 1)
                q[par, u, f, row, 1] = jnp.where(low_half, near_low, roll_s(q[par, u, f, row, 5], 1))
                q[par, u, f, row, 6] = jnp.where(low_half, roll_s(q[par, u, f, row, 2], -1), near_high)

    def sent_halos(par, u):
        for part in ("corner", "inner", "outer"):
            for copy, sends, _ in halo_copies(par, u, part):
                guarded(sends, copy.wait_send)

    def tendency(ref, u, row, z, cos, sin, scale):
        center, gx, gy, gz, laplace = [], [], [], [], []
        for f in range(4):
            c = ref[f, row, z]
            north, south = ref[f, row + 1, z], ref[f, row - 1, z]
            upper, lower = ref[f, row, z + 1], ref[f, row, z - 1]
            east, west = pltpu.roll(c, 127, 1), pltpu.roll(c, 1, 1)
            east = jnp.where(last_lane, roll_s(east, -2), east)
            west = jnp.where(first_lane, roll_s(west, 2), west)
            center.append(c)
            gx.append(east - west)
            gy.append(north - south)
            gz.append(upper - lower)
            laplace.append(((east + west) + (north + south)) + (upper + lower) - 6.0 * c)
        strain = gx[1] * gx[1] + gy[2] * gy[2] + gz[3] * gz[3] + gy[1] * gy[1] + gz[1] * gz[1]
        viscous = (0.5 * scale * VISC) * jnp.sqrt(4.0 + strain)
        speed = 1.0 + center[1]
        half = 0.5 * scale
        half_u, half_v, half_w = half * speed, half * center[2], half * center[3]
        normal = speed * cos + center[2] * sin
        kind = 0 if z == 1 else 2 if z == 6 else 1
        thrust = normal * jnp.abs(normal) * (scale * weight[u, kind, row])
        extra = [
            half * (gx[1] + gy[2] + gz[3]),
            half * gx[0] + thrust * cos,
            half * gy[0] + thrust * sin,
            half * gz[0],
        ]
        rates = [
            viscous * laplace[f] - (half_u * gx[f] + half_v * gy[f] + half_w * gz[f] + extra[f])
            for f in range(4)
        ]
        return center, rates

    def fringe_copy(s, chunk):
        part = fringe.at[s, pl.ds(*((1, 3), (4, 3), (0, 1), (7, 1))[chunk])]
        return pltpu.make_async_remote_copy(
            src_ref=part, dst_ref=part, send_sem=fs.at[s, chunk], recv_sem=fr.at[s, chunk],
            device_id={"case": lax.rem(case + 1, n_case)}, device_id_type=MESH,
        )

    def pack_fringe(nxt, s, start, stop, step, chunks):
        @pl.loop(start, stop, step=step)
        def _(y):
            for f in range(4):
                parts = [q[nxt, 0, f, y + 2, 2 + k] for k in range(4)]
                parts = [parts[0]] + [roll_s(parts[k], 2 * k) for k in (1, 2, 3)]
                fringe[s, y, f] = jnp.where(
                    sub < 4, jnp.where(sub < 2, parts[0], parts[1]), jnp.where(sub < 6, parts[2], parts[3])
                )

        for chunk in chunks:
            fringe_copy(s, chunk).start()

    def advance(par, nxt, u, s):
        cos, sin = angle_cos[u], angle_sin[u]
        field = q.at[par, u]

        def first(row, zs):
            for z in zs:
                center, rates = tendency(field, u, row, z, cos, sin, TIME_STEP)
                for f in range(4):
                    value = center[f] + rates[f]
                    if z == 1:
                        value = jnp.where(low_half & edge_low, 0.0, value)
                    if z == 6:
                        value = jnp.where(jnp.logical_not(low_half) & edge_high, 0.0, value)
                    mid[f, row, z] = value

        edge_low = jnp.full((8, 128), vert, jnp.int32) == 0
        edge_high = jnp.full((8, 128), vert, jnp.int32) == n_vert - 1

        for row in range(3, 9):
            first(row, (3, 4))

        receive_inner(par, u)

        first(2, range(2, 6))
        first(9, range(2, 6))

        for row in range(3, 9):
            first(row, (2, 5))

        receive_outer(par, u)

        first(1, (3, 4))
        first(10, (3, 4))

        for row in range(3, 9):
            first(row, (1, 6))

        def second(row, zs):
            for z in zs:
                center, rates = tendency(mid, u, row, z, cos, sin, 0.5 * TIME_STEP)
                for f in range(4):
                    q[nxt, u, f, row, z] = 0.5 * (field[f, row, z] + center[f]) + rates[f]

        pl.when((s > 0) & ((u == 1) | (s != 1)))(lambda: sent_halos(1 - par, u))

        for row in range(3, 9):
            second(row, range(2, 6))

        @pl.when((case == 0) & (u == 0))
        def _():
            pack_fringe(nxt, s, 1, 7, 1, (0, 1))

        second(2, (3, 4))
        second(9, (3, 4))

        receive_corners(par, u)

        for row, z in ((1, 2), (1, 5), (10, 2), (10, 5), (2, 1), (2, 6), (9, 1), (9, 6)):
            first(row, (z,))
        for row, z in ((2, 2), (2, 5), (9, 2), (9, 5)):
            second(row, (z,))

    def blend(nxt, u, s):
        ramp = ramp_ref[...]

        @pl.loop(0, 8)
        def _(y):
            for f in range(4):
                packed = fringe[s, y, f]
                for k in range(4):
                    value = q[nxt, u, f, y + 2, 2 + k]
                    q[nxt, u, f, y + 2, 2 + k] = value + ramp * (roll_s(packed, -2 * k) - value)

    def copy_out(u):
        return pltpu.make_async_copy(stage.at[u], out_ref.at[u], load_sem.at[u])

    def emit(nxt, u, blended):
        ramp = ramp_ref[...]

        @pl.loop(0, 8)
        def _(y):
            for f in range(4):
                packed = fringe[STEPS - 1, y, f]
                for k in range(4):
                    value = q[nxt, u, f, y + 2, 2 + k]
                    if blended:
                        value = value + ramp * (roll_s(packed, -2 * k) - value)
                    stage[u, f, y, pl.ds(k, 8, stride=4), :] = value

        copy_out(u).start()

    for u in (0, 1):
        loads[u].wait()

        @pl.loop(0, 8)
        def _(y):
            for f in range(4):
                for k in range(4):
                    q[0, u, f, y + 2, 2 + k] = stage[u, f, y, pl.ds(k, 8, stride=4), :]

        if u == 0:
            pl.semaphore_wait(barrier, len(partners))
        if u == 1:
            sent_halos(0, 0)
        send_halos(0, u)

    constants()

    @pl.loop(0, 2 * STEPS)
    def _(task):
        u, s = lax.rem(task, 2), lax.div(task, 2)
        par = lax.rem(s, 2)
        nxt = 1 - par
        more = s < STEPS - 1
        first_slot = u == 0
        early = ((s > 0) | (case == 1)) & ((s < STEPS - 1) | (case < n_case - 1))

        advance(par, nxt, u, s)

        @pl.when((case == 0) & first_slot)
        def _():
            pack_fringe(nxt, s, 0, 8, 7, (2, 3))
            pl.when(jnp.logical_not(more))(lambda: emit(nxt, 0, False))

        @pl.when((case > 0) & (first_slot == early))
        def _():
            for chunk in range(4):
                fringe_copy(s, chunk).wait_recv()
                pl.when(case < n_case - 1)(fringe_copy(s, chunk).start)
            pl.when(more)(lambda: blend(nxt, 0, s))
            pl.when(jnp.logical_not(more))(lambda: emit(nxt, 0, True))

        @pl.when(more & ((case == 0) & first_slot | (case > 0) & (first_slot == early)))
        def _():
            send_halos(nxt, 0)

        @pl.when(jnp.logical_not(first_slot) & more)
        def _():
            blend(nxt, 1, s)
            send_halos(nxt, 1)

        @pl.when(jnp.logical_not(first_slot | more))
        def _():
            emit(nxt, 1, True)

    @pl.when(case < n_case - 1)
    def _():
        for s in range(STEPS):
            for f in range(4):
                fringe_copy(s, f).wait_send()

    for u in (0, 1):
        sent_halos((STEPS - 1) % 2, u)
    for u in (0, 1):
        copy_out(u).wait()


def body(state, turbine_x, turbine_y, yaw_index):
    slots, fields, rows_y, rows_z, x = state.shape
    tiles = x // 128
    tiled = state.reshape(slots, fields, rows_y, rows_z, tiles, 128).transpose(0, 1, 2, 4, 3, 5)
    tiled = tiled.reshape(slots, fields, rows_y, tiles * rows_z, 128)
    domain = (2, 4, 12, 8, 8, 128)
    out = pl.pallas_call(
        kernel,
        out_shape=jax.ShapeDtypeStruct(tiled.shape, jnp.float32),
        in_specs=[pl.BlockSpec(memory_space=pltpu.HBM)] + [pl.BlockSpec(memory_space=pltpu.HBM)] * 3,
        out_specs=pl.BlockSpec(memory_space=pltpu.HBM),
        scratch_shapes=[
            pltpu.VMEM(tiled.shape, jnp.float32),
            pltpu.VMEM((2,) + domain, jnp.float32),
            pltpu.VMEM(domain[1:], jnp.float32),
            pltpu.VMEM((2, 2, 2, 2, 4, 4, 8, 128), jnp.float32),
            pltpu.VMEM((2, 2, 2, 2, 4, 4, 8, 128), jnp.float32),
            pltpu.VMEM((2, 2, 4, 2, 8, 128), jnp.float32),
            pltpu.VMEM((2, 2, 4, 2, 8, 128), jnp.float32),
            pltpu.VMEM((STEPS, 8, 4, 8, 128), jnp.float32),
            pltpu.VMEM((2, 3, 12, 8, 128), jnp.float32),
            pltpu.VMEM((2, 8, 128), jnp.float32),
            pltpu.VMEM((2, 8, 128), jnp.float32),
            pltpu.VMEM((8, 128), jnp.float32),
            pltpu.SMEM(turbine_x.shape, jnp.int32),
            pltpu.SMEM(turbine_y.shape, jnp.int32),
            pltpu.SMEM(yaw_index.shape, jnp.int32),
            pltpu.SemaphoreType.DMA((5,)),
            pltpu.SemaphoreType.DMA((2, 2, 12)),
            pltpu.SemaphoreType.DMA((2, 2, 12)),
            pltpu.SemaphoreType.DMA((STEPS, 4)),
            pltpu.SemaphoreType.DMA((STEPS, 4)),
        ],
        compiler_params=pltpu.CompilerParams(
            collective_id=0, has_side_effects=True, vmem_limit_bytes=60 << 20
        ),
        name="heun_steps",
    )(tiled, turbine_x, turbine_y, yaw_index)
    out = out.reshape(slots, fields, rows_y, tiles, rows_z, 128).transpose(0, 1, 2, 4, 3, 5)
    return out.reshape(state.shape)


def solution(mesh):
    return jax.shard_map(
        body,
        mesh=mesh,
        in_specs=(
            P("case", None, "span", "vert", None),
            P("case", None),
            P("case", None),
            P("case"),
        ),
        out_specs=P("case", None, "span", "vert", None),
        check_vma=False,
    )
```

```python
import functools
import math

import jax
import jax.numpy as jnp
from jax import lax
from jax.experimental import pallas as pl
from jax.experimental.pallas import tpu as pltpu
from jax.sharding import PartitionSpec as P

STEPS = 3
DISK = 8
VISC = 0.04
THRUST = 0.75
TIME_STEP = 0.1
YAW_STEP = 0.15
MESH = pl.DeviceIdType.MESH

OWN = slice(2, 6)


def roll_s(v, shift):
    return pltpu.roll(v, shift % 8, 0)


def kernel(
    state_ref, tx_hbm, ty_hbm, yaw_hbm, out_ref,
    stage, q, mid, send_z, recv_z, send_c, recv_c, fringe, weight, angle_cos, angle_sin, ramp_ref, tx_ref, ty_ref, yaw_ref,
    load_sem, hs, hr, fs, fr,
):
    case, span, vert = lax.axis_index("case"), lax.axis_index("span"), lax.axis_index("vert")
    n_case, n_span, n_vert = lax.axis_size("case"), lax.axis_size("span"), lax.axis_size("vert")
    left, right = lax.rem(span + n_span - 1, n_span), lax.rem(span + 1, n_span)
    below, above = lax.rem(vert + n_vert - 1, n_vert), lax.rem(vert + 1, n_vert)
    has_below, has_above = vert > 0, vert < n_vert - 1
    total_y, half_z = 8 * n_span, 4 * n_vert

    loads = [
        pltpu.make_async_copy(state_ref.at[u], stage.at[u], load_sem.at[u]) for u in (0, 1)
    ]
    loads += [
        pltpu.make_async_copy(src, dst, load_sem.at[2 + i])
        for i, (src, dst) in enumerate(((tx_hbm, tx_ref), (ty_hbm, ty_ref), (yaw_hbm, yaw_ref)))
    ]
    barrier = pltpu.get_barrier_semaphore()
    partners = [
        {"span": s, "vert": v} for s in (left, span, right) for v in (below, vert, above)
    ]
    partners.pop(4)
    partners += [{"case": lax.rem(case + k, n_case)} for k in (1, n_case - 1)]
    for partner in partners:
        pl.semaphore_signal(barrier, inc=1, device_id=partner, device_id_type=MESH)
    for copy in loads:
        copy.start()

    sub = lax.broadcasted_iota(jnp.int32, (8, 128), 0)
    lane = lax.broadcasted_iota(jnp.int32, (8, 128), 1)
    low_half = (sub & 1) == 0
    first_lane, last_lane = lane == 0, lane == 127
    along_x = (sub >> 1) * 128 + lane

    zeros = jnp.zeros((8, 128), jnp.float32)

    def constants():
        for copy in loads[2:]:
            copy.wait()
        wave = jnp.cos((math.pi / 128.0) * (along_x + 1).astype(jnp.float32))
        ramp_ref[...] = jnp.where(sub < 2, 0.5 * (1.0 - wave), 0.0)
        half = jnp.where(low_half, 0, 4)
        for u in (0, 1):
            yaw = jnp.full((8, 128), yaw_ref[u], jnp.int32).astype(jnp.float32)
            angle = (yaw - 3.5) * YAW_STEP
            angle_cos[u] = jnp.cos(angle)
            angle_sin[u] = jnp.sin(angle)

            @pl.loop(1, 11)
            def _(row):
                y = span * 8 + row - 2
                total = zeros
                for k in range(tx_ref.shape[1]):
                    offset = jnp.full((8, 128), y - ty_ref[u, k], jnp.int32) & (total_y - 1)
                    hit = (along_x == tx_ref[u, k]) & (offset < DISK)
                    total = total + jnp.where(hit, THRUST, 0.0)
                domain = jnp.full((8, 128), 2 * case + u, jnp.int32)
                for kind, z in enumerate((1, 2, 6)):
                    height = half + (vert * 8 + z - 2)
                    weight[u, kind, row] = jnp.where((height < half_z) & (domain > 0), total, 0.0)

        @pl.when(jnp.logical_not(has_below))
        def _():
            @pl.loop(0, 4)
            def _(y):
                for par in (0, 1):
                    for u in (0, 1):
                        for f in range(4):
                            recv_z[par, u, 0, 0, f, y] = zeros
                            recv_z[par, u, 0, 1, f, y] = zeros
            for par in (0, 1):
                for u in (0, 1):
                    for f in range(2):
                        recv_c[par, u, 0, f] = zeros
                        recv_c[par, u, 2, f] = zeros

        @pl.when(jnp.logical_not(has_above))
        def _():
            @pl.loop(0, 4)
            def _(y):
                for par in (0, 1):
                    for u in (0, 1):
                        for f in range(4):
                            recv_z[par, u, 1, 0, f, y] = zeros
                            recv_z[par, u, 1, 1, f, y] = zeros
            for par in (0, 1):
                for u in (0, 1):
                    for f in range(2):
                        recv_c[par, u, 1, f] = zeros
                        recv_c[par, u, 3, f] = zeros

    def remote(src, dst, par, u, k, device):
        return pltpu.make_async_remote_copy(
            src_ref=src, dst_ref=dst, send_sem=hs.at[par, u, k], recv_sem=hr.at[par, u, k],
            device_id=device, device_id_type=MESH,
        )

    def halo_copies(par, u, part):
        own = q.at[par, u]
        if part == "corner":
            return [
                (remote(send_c.at[par, u, 0], recv_c.at[par, u, 0], par, u, 4, {"span": right, "vert": above}), has_above, has_below),
                (remote(send_c.at[par, u, 1], recv_c.at[par, u, 1], par, u, 5, {"span": right, "vert": below}), has_below, has_above),
                (remote(send_c.at[par, u, 2], recv_c.at[par, u, 2], par, u, 6, {"span": left, "vert": above}), has_above, has_below),
                (remote(send_c.at[par, u, 3], recv_c.at[par, u, 3], par, u, 7, {"span": left, "vert": below}), has_below, has_above),
            ]
        if part == "inner":
            return [
                (remote(send_z.at[par, u, 0, 0], recv_z.at[par, u, 0, 0], par, u, 0, {"vert": above}), has_above, has_below),
                (remote(send_z.at[par, u, 1, 0], recv_z.at[par, u, 1, 0], par, u, 1, {"vert": below}), has_below, has_above),
                (remote(own.at[:, 9, OWN], own.at[:, 1, OWN], par, u, 2, {"span": right}), None, None),
                (remote(own.at[:, 2, OWN], own.at[:, 10, OWN], par, u, 3, {"span": left}), None, None),
            ]
        return [
            (remote(send_z.at[par, u, 0, 1], recv_z.at[par, u, 0, 1], par, u, 8, {"vert": above}), has_above, has_below),
            (remote(send_z.at[par, u, 1, 1], recv_z.at[par, u, 1, 1], par, u, 9, {"vert": below}), has_below, has_above),
            (remote(own.at[:, 8, OWN], own.at[:, 0, OWN], par, u, 10, {"span": right}), None, None),
            (remote(own.at[:, 3, OWN], own.at[:, 11, OWN], par, u, 11, {"span": left}), None, None),
        ]

    def guarded(condition, action):
        if condition is None:
            action()
        else:
            pl.when(condition)(action)

    def send_halos(par, u):
        for k, (row, z) in enumerate(((9, 5), (9, 2), (2, 5), (2, 2))):
            for f in (0, 2):
                even, odd = q[par, u, f, row, z], q[par, u, f + 1, row, z]
                pair = (roll_s(even, -1), odd) if z == 5 else (even, roll_s(odd, 1))
                send_c[par, u, k, f // 2] = jnp.where(low_half, *pair)
        for copy, sends, _ in halo_copies(par, u, "corner"):
            guarded(sends, copy.start)

        for part in ("inner", "outer"):
            for copy, _, _ in halo_copies(par, u, part)[2:]:
                copy.start()

        @pl.loop(0, 4)
        def _(y):
            for f in range(4):
                even = [q[par, u, f, 2 * y + 2, z] for z in range(2, 6)]
                odd = [q[par, u, f, 2 * y + 3, z] for z in range(2, 6)]
                send_z[par, u, 0, 0, f, y] = jnp.where(low_half, roll_s(even[3], -1), odd[3])
                send_z[par, u, 0, 1, f, y] = jnp.where(low_half, roll_s(even[2], -1), odd[2])
                send_z[par, u, 1, 0, f, y] = jnp.where(low_half, even[0], roll_s(odd[0], 1))
                send_z[par, u, 1, 1, f, y] = jnp.where(low_half, even[1], roll_s(odd[1], 1))

        for part in ("inner", "outer"):
            for copy, sends, _ in halo_copies(par, u, part)[:2]:
                guarded(sends, copy.start)

    def merge_z(par, u, layer):
        @pl.loop(0, 4)
        def _(y):
            for f in range(4):
                low, high = recv_z[par, u, 0, layer, f, y], recv_z[par, u, 1, layer, f, y]
                for odd in (0, 1):
                    row = 2 * y + 2 + odd
                    near_low, near_high = q[par, u, f, row, 5 - layer], q[par, u, f, row, 2 + layer]
                    q[par, u, f, row, 1 - layer] = jnp.where(low_half, roll_s(low, -1) if odd else low, roll_s(near_low, 1))
                    q[par, u, f, row, 6 + layer] = jnp.where(low_half, roll_s(near_high, -1), high if odd else roll_s(high, 1))

    def receive_inner(par, u):
        for copy, _, receives in halo_copies(par, u, "inner"):
            guarded(receives, copy.wait_recv)
        merge_z(par, u, 0)

    def receive_outer(par, u):
        for copy, _, receives in halo_copies(par, u, "outer"):
            guarded(receives, copy.wait_recv)
        merge_z(par, u, 1)

    def receive_corners(par, u):
        for copy, _, receives in halo_copies(par, u, "corner"):
            guarded(receives, copy.wait_recv)
        for f in range(4):
            for row, low, high in ((1, 0, 1), (10, 2, 3)):
                near_low, near_high = recv_c[par, u, low, f // 2], recv_c[par, u, high, f // 2]
                if f % 2:
                    near_low = roll_s(near_low, -1)
                else:
                    near_high = roll_s(near_high, 1)
                q[par, u, f, row, 1] = jnp.where(low_half, near_low, roll_s(q[par, u, f, row, 5], 1))
                q[par, u, f, row, 6] = jnp.where(low_half, roll_s(q[par, u, f, row, 2], -1), near_high)

    def sent_halos(par, u):
        for part in ("corner", "inner", "outer"):
            for copy, sends, _ in halo_copies(par, u, part):
                guarded(sends, copy.wait_send)

    def tendency(ref, u, row, z, cos, sin, scale):
        center, gx, gy, gz, laplace = [], [], [], [], []
        for f in range(4):
            c = ref[f, row, z]
            north, south = ref[f, row + 1, z], ref[f, row - 1, z]
            upper, lower = ref[f, row, z + 1], ref[f, row, z - 1]
            east, west = pltpu.roll(c, 127, 1), pltpu.roll(c, 1, 1)
            east = jnp.where(last_lane, roll_s(east, -2), east)
            west = jnp.where(first_lane, roll_s(west, 2), west)
            center.append(c)
            gx.append(east - west)
            gy.append(north - south)
            gz.append(upper - lower)
            laplace.append(((east + west) + (north + south)) + (upper + lower) - 6.0 * c)
        strain = gx[1] * gx[1] + gy[2] * gy[2] + gz[3] * gz[3] + gy[1] * gy[1] + gz[1] * gz[1]
        viscous = (0.5 * scale * VISC) * jnp.sqrt(4.0 + strain)
        speed = 1.0 + center[1]
        half = 0.5 * scale
        half_u, half_v, half_w = half * speed, half * center[2], half * center[3]
        normal = speed * cos + center[2] * sin
        kind = 0 if z == 1 else 2 if z == 6 else 1
        thrust = normal * jnp.abs(normal) * (scale * weight[u, kind, row])
        extra = [
            half * (gx[1] + gy[2] + gz[3]),
            half * gx[0] + thrust * cos,
            half * gy[0] + thrust * sin,
            half * gz[0],
        ]
        rates = [
            viscous * laplace[f] - (half_u * gx[f] + half_v * gy[f] + half_w * gz[f] + extra[f])
            for f in range(4)
        ]
        return center, rates

    def fringe_copy(s, chunk):
        part = fringe.at[s, pl.ds(*((1, 3), (4, 3), (0, 1), (7, 1))[chunk])]
        return pltpu.make_async_remote_copy(
            src_ref=part, dst_ref=part, send_sem=fs.at[s, chunk], recv_sem=fr.at[s, chunk],
            device_id={"case": lax.rem(case + 1, n_case)}, device_id_type=MESH,
        )

    def pack_fringe(nxt, s, start, stop, step, chunks):
        @pl.loop(start, stop, step=step)
        def _(y):
            for f in range(4):
                parts = [q[nxt, 0, f, y + 2, 2 + k] for k in range(4)]
                parts = [parts[0]] + [roll_s(parts[k], 2 * k) for k in (1, 2, 3)]
                fringe[s, y, f] = jnp.where(
                    sub < 4, jnp.where(sub < 2, parts[0], parts[1]), jnp.where(sub < 6, parts[2], parts[3])
                )

        for chunk in chunks:
            fringe_copy(s, chunk).start()

    def advance(par, nxt, u, s):
        cos, sin = angle_cos[u], angle_sin[u]
        field = q.at[par, u]

        def first(row, zs):
            for z in zs:
                center, rates = tendency(field, u, row, z, cos, sin, TIME_STEP)
                for f in range(4):
                    value = center[f] + rates[f]
                    if z == 1:
                        value = jnp.where(low_half & edge_low, 0.0, value)
                    if z == 6:
                        value = jnp.where(jnp.logical_not(low_half) & edge_high, 0.0, value)
                    mid[f, row, z] = value

        edge_low = jnp.full((8, 128), vert, jnp.int32) == 0
        edge_high = jnp.full((8, 128), vert, jnp.int32) == n_vert - 1

        for row in range(3, 9):
            first(row, (3, 4))

        receive_inner(par, u)

        first(2, range(2, 6))
        first(9, range(2, 6))

        for row in range(3, 9):
            first(row, (2, 5))

        receive_outer(par, u)

        first(1, (3, 4))
        first(10, (3, 4))

        for row in range(3, 9):
            first(row, (1, 6))

        def second(row, zs):
            for z in zs:
                center, rates = tendency(mid, u, row, z, cos, sin, 0.5 * TIME_STEP)
                for f in range(4):
                    q[nxt, u, f, row, z] = 0.5 * (field[f, row, z] + center[f]) + rates[f]

        pl.when((s > 0) & ((u == 1) | (s != 1)))(lambda: sent_halos(1 - par, u))

        for start, chunk in ((3, 0), (6, 1)):
            for row in range(start, start + 3):
                second(row, range(2, 6))

            @pl.when((case == 0) & (u == 0))
            def _():
                pack_fringe(nxt, s, start - 2, start + 1, 1, (chunk,))

        second(2, (3, 4))
        second(9, (3, 4))

        receive_corners(par, u)

        for row, z in ((1, 2), (1, 5), (10, 2), (10, 5), (2, 1), (2, 6), (9, 1), (9, 6)):
            first(row, (z,))
        for row, z in ((2, 2), (2, 5), (9, 2), (9, 5)):
            second(row, (z,))

    def blend(nxt, u, s, start=0, stop=8):
        ramp = ramp_ref[...]

        @pl.loop(start, stop)
        def _(y):
            for f in range(4):
                packed = fringe[s, y, f]
                for k in range(4):
                    value = q[nxt, u, f, y + 2, 2 + k]
                    q[nxt, u, f, y + 2, 2 + k] = value + ramp * (roll_s(packed, -2 * k) - value)

    def copy_out(u):
        return pltpu.make_async_copy(stage.at[u], out_ref.at[u], load_sem.at[u])

    def emit(nxt, u, blended):
        ramp = ramp_ref[...]

        @pl.loop(0, 8)
        def _(y):
            for f in range(4):
                packed = fringe[STEPS - 1, y, f]
                for k in range(4):
                    value = q[nxt, u, f, y + 2, 2 + k]
                    if blended:
                        value = value + ramp * (roll_s(packed, -2 * k) - value)
                    stage[u, f, y, pl.ds(k, 8, stride=4), :] = value

        copy_out(u).start()

    for u in (0, 1):
        loads[u].wait()

        @pl.loop(0, 8)
        def _(y):
            for f in range(4):
                for k in range(4):
                    q[0, u, f, y + 2, 2 + k] = stage[u, f, y, pl.ds(k, 8, stride=4), :]

        if u == 0:
            pl.semaphore_wait(barrier, len(partners))
        if u == 1:
            sent_halos(0, 0)
        send_halos(0, u)

    constants()

    @pl.loop(0, 2 * STEPS)
    def _(task):
        u, s = lax.rem(task, 2), lax.div(task, 2)
        par = lax.rem(s, 2)
        nxt = 1 - par
        more = s < STEPS - 1
        first_slot = u == 0
        early = ((s > 0) | (case < 3)) & ((s < STEPS - 1) | (case < n_case - 1))

        advance(par, nxt, u, s)

        @pl.when((case == 0) & first_slot)
        def _():
            pack_fringe(nxt, s, 0, 8, 7, (2, 3))
            pl.when(jnp.logical_not(more))(lambda: emit(nxt, 0, False))

        @pl.when((case > 0) & (first_slot == early))
        def _():
            for chunk, (start, stop) in enumerate(((1, 4), (4, 7), (0, 1), (7, 8))):
                fringe_copy(s, chunk).wait_recv()
                pl.when(case < n_case - 1)(fringe_copy(s, chunk).start)
                if chunk < 2:
                    blend(nxt, 0, s, start, stop)
            blend(nxt, 0, s, 0, 1)
            blend(nxt, 0, s, 7, 8)
            pl.when(jnp.logical_not(more))(lambda: emit(nxt, 0, False))

        @pl.when(more & ((case == 0) & first_slot | (case > 0) & (first_slot == early)))
        def _():
            send_halos(nxt, 0)

        @pl.when(jnp.logical_not(first_slot) & more)
        def _():
            blend(nxt, 1, s)
            send_halos(nxt, 1)

        @pl.when(jnp.logical_not(first_slot | more))
        def _():
            emit(nxt, 1, True)

    @pl.when(case < n_case - 1)
    def _():
        for s in range(STEPS):
            for f in range(4):
                fringe_copy(s, f).wait_send()

    for u in (0, 1):
        sent_halos((STEPS - 1) % 2, u)
    for u in (0, 1):
        copy_out(u).wait()


def body(state, turbine_x, turbine_y, yaw_index):
    slots, fields, rows_y, rows_z, x = state.shape
    tiles = x // 128
    tiled = state.reshape(slots, fields, rows_y, rows_z, tiles, 128).transpose(0, 1, 2, 4, 3, 5)
    tiled = tiled.reshape(slots, fields, rows_y, tiles * rows_z, 128)
    domain = (2, 4, 12, 8, 8, 128)
    out = pl.pallas_call(
        kernel,
        out_shape=jax.ShapeDtypeStruct(tiled.shape, jnp.float32),
        in_specs=[pl.BlockSpec(memory_space=pltpu.HBM)] + [pl.BlockSpec(memory_space=pltpu.HBM)] * 3,
        out_specs=pl.BlockSpec(memory_space=pltpu.HBM),
        scratch_shapes=[
            pltpu.VMEM(tiled.shape, jnp.float32),
            pltpu.VMEM((2,) + domain, jnp.float32),
            pltpu.VMEM(domain[1:], jnp.float32),
            pltpu.VMEM((2, 2, 2, 2, 4, 4, 8, 128), jnp.float32),
            pltpu.VMEM((2, 2, 2, 2, 4, 4, 8, 128), jnp.float32),
            pltpu.VMEM((2, 2, 4, 2, 8, 128), jnp.float32),
            pltpu.VMEM((2, 2, 4, 2, 8, 128), jnp.float32),
            pltpu.VMEM((STEPS, 8, 4, 8, 128), jnp.float32),
            pltpu.VMEM((2, 3, 12, 8, 128), jnp.float32),
            pltpu.VMEM((2, 8, 128), jnp.float32),
            pltpu.VMEM((2, 8, 128), jnp.float32),
            pltpu.VMEM((8, 128), jnp.float32),
            pltpu.SMEM(turbine_x.shape, jnp.int32),
            pltpu.SMEM(turbine_y.shape, jnp.int32),
            pltpu.SMEM(yaw_index.shape, jnp.int32),
            pltpu.SemaphoreType.DMA((5,)),
            pltpu.SemaphoreType.DMA((2, 2, 12)),
            pltpu.SemaphoreType.DMA((2, 2, 12)),
            pltpu.SemaphoreType.DMA((STEPS, 4)),
            pltpu.SemaphoreType.DMA((STEPS, 4)),
        ],
        compiler_params=pltpu.CompilerParams(
            collective_id=0, has_side_effects=True, vmem_limit_bytes=60 << 20
        ),
        name="heun_steps",
    )(tiled, turbine_x, turbine_y, yaw_index)
    out = out.reshape(slots, fields, rows_y, tiles, rows_z, 128).transpose(0, 1, 2, 4, 3, 5)
    return out.reshape(state.shape)


def solution(mesh):
    return jax.shard_map(
        body,
        mesh=mesh,
        in_specs=(
            P("case", None, "span", "vert", None),
            P("case", None),
            P("case", None),
            P("case"),
        ),
        out_specs=P("case", None, "span", "vert", None),
        check_vma=False,
    )
```
